256 devices in a mesh: samp: 16 (over y, x_lo, core), var: 16 (over z, x_hi).
Axes of the slice: x: 4 (x_hi: 2, x_lo: 2; x = x_hi * 2 + x_lo), y: 4, z: 8, core: 2. Of those that a mesh axis runs over, the one named last changes fastest.
Arguments:
- dosage: bfloat16 [10752, 8192], P('samp', 'var'), may hold values from 0 to 2
- cohort: int32 [10752], P('samp'), may hold values from 0 to 7, as said below
- live_blocks: int32 [16], P('samp'), may hold values from 1 to 7, as said below
- weight_counts: int32 [8], replicated, may hold values from 50 to 1999
Outputs:
- ld_matrix: float32 [8192, 8192], P('samp', 'var')
The draws below stay inside these ranges and needn't reach their ends.
Inputs may be any that keep to these rules, and one draw needn't show every extreme that they name: Every cohort has a live sample on every sample-axis device. live_blocks[i] + live_blocks[i + N/2] = 8 for every i below N/2, N the length of live_blocks; some device has 7.
All inputs are finite; a program needn't handle non-finite values.
Results may differ from the reference program's by a relative error of at most 0.0032.
Values may be sent and summed in bfloat16 or wider, within the bound.
A program may use at most 128 MiB of HBM per device.

```python
import jax
import jax.numpy as jnp
from jax import lax

V = 8192
COHORTS = 8
BLOCK = 96
HALF = 4
CAP = 7
SAMPLES = 10752
N_SAMP = 16


def cohort_labels(key):
    base = jax.random.fold_in(key, 71)
    drawn = jax.random.randint(base, (SAMPLES,), 0, COHORTS)
    position = jnp.arange(SAMPLES, dtype=jnp.int32) % (CAP * BLOCK)
    return jnp.where(position < COHORTS, position, drawn).astype(jnp.int32)


def draw_cohort(key, part):
    return cohort_labels(key)


def draw_dosage(key, part):
    labels = cohort_labels(key)
    keys = jax.random.split(jax.random.fold_in(key, 5), 4)
    noise = jax.random.normal(keys[0], (SAMPLES, V), jnp.float32)
    lag_one = jax.random.uniform(keys[1], (COHORTS, V), jnp.float32, -0.9, 0.9)
    lag_two = jax.random.uniform(keys[2], (COHORTS, V), jnp.float32, -0.5, 0.5)
    offsets = jax.random.uniform(keys[3], (COHORTS, V), jnp.float32, -1.5, 1.5)
    zero_col = jnp.zeros((SAMPLES, 1), jnp.float32)
    shift_one = jnp.concatenate([zero_col, noise[:, :-1]], axis=1)
    shift_two = jnp.concatenate([zero_col, shift_one[:, :-1]], axis=1)
    latent = noise + lag_one[labels] * shift_one + lag_two[labels] * shift_two
    dosage = 2.0 * jax.nn.sigmoid(0.9 * latent + offsets[labels])
    return dosage.astype(jnp.bfloat16)


def draw_live_blocks(key, part):
    keys = jax.random.split(jax.random.fold_in(key, 13), 3)
    pair_count = N_SAMP // 2
    lower = jax.random.randint(keys[0], (pair_count,), 1, 2 * HALF)
    chosen = jax.random.randint(keys[1], (), 0, pair_count)
    lower = jnp.where(jnp.arange(pair_count) == chosen, CAP, lower)
    flipped = jax.random.randint(keys[2], (pair_count,), 0, 2)
    first_half = jnp.where(flipped == 1, lower, 2 * HALF - lower)
    return jnp.concatenate([first_half, 2 * HALF - first_half]).astype(jnp.int32)


def set_ends(entries, rng, low, largest):
    longest = entries.shape.index(max(entries.shape))
    spots = []
    for shift in (0, 1):
        where = [jax.random.randint(jax.random.fold_in(rng, axis), (), 0, length) for axis, length in enumerate(entries.shape)]
        where[longest] = (where[longest] + shift) % entries.shape[longest]
        spots.append(tuple(where))
    return entries.at[spots[0]].set(low).at[spots[1]].set(largest)


def setup_inputs(seed: int = 0) -> dict:
    key_of = jax.random.split(jax.random.key(seed), 5)
    dosage = draw_dosage(jax.random.fold_in(key_of[4], 71), 0)
    cohort = draw_cohort(jax.random.fold_in(key_of[4], 71), 0)
    live_blocks = draw_live_blocks(jax.random.fold_in(key_of[4], 71), 0)
    weight_counts = set_ends(jax.random.randint(key_of[3], (COHORTS,), 50, 2000), jax.random.fold_in(key_of[3], 1), 50, 1999).astype(jnp.int32)
    return dict(dosage=dosage, cohort=cohort, live_blocks=live_blocks, weight_counts=weight_counts)


EPSILON = 1e-05

def reference(dosage, cohort, live_blocks, weight_counts):
    slot_count = CAP * BLOCK
    position = jnp.arange(SAMPLES, dtype=jnp.int32)
    owner_live = jnp.repeat(live_blocks, slot_count, total_repeat_length=SAMPLES)
    live_mask = (position % slot_count // BLOCK < owner_live).astype(jnp.float32)
    cohort_codes = jnp.arange(COHORTS, dtype=jnp.int32)
    member = jnp.where(cohort[None, :] == cohort_codes[:, None], live_mask[None, :], 0.0).astype(jnp.float32)
    values = dosage.astype(jnp.float32)
    sum_one = jnp.dot(member, values, precision=lax.Precision.HIGHEST)
    sum_two = jnp.dot(member, values * values, precision=lax.Precision.HIGHEST)
    cohort_size = lax.optimization_barrier(jnp.sum(member, axis=1))
    cohort_mean = sum_one / cohort_size[:, None]
    cohort_var = sum_two / cohort_size[:, None] - cohort_mean * cohort_mean
    inv_spread = lax.rsqrt(cohort_var + EPSILON)
    counts_float = weight_counts.astype(jnp.float32)
    cohort_share = counts_float / jnp.sum(counts_float)
    cohort_scale = jnp.sqrt(cohort_share / cohort_size)
    multiplier = inv_spread * cohort_scale[:, None]
    centered = values - cohort_mean[cohort]
    scaled = (live_mask[:, None] * centered * multiplier[cohort]).astype(jnp.bfloat16)
    grouped = scaled.reshape(N_SAMP, slot_count, V)

    def add_group(total, rows):
        partial_value = jnp.dot(rows.T, rows, preferred_element_type=jnp.float32)
        return (total + partial_value, None)
    result, unused = lax.scan(add_group, jnp.zeros((V, V), jnp.float32), grouped)
    return result
```

```python
import jax
import jax.numpy as jnp
from jax import lax
from jax.experimental import pallas as pl
from jax.experimental.pallas import tpu as pltpu
from jax.sharding import Mesh
from jax.sharding import PartitionSpec as P

COHORTS = 8
BLOCK = 96
HALF = 4
ROWS = HALF * BLOCK
SURPLUS = 3 * BLOCK
LANES = 128
PANEL = 512
DEPTH = 4 * ROWS
EPSILON = 1e-05
MESH = pl.DeviceIdType.MESH
F32 = jnp.float32
BF16 = jnp.bfloat16


def split_three(value):
    first = value.astype(BF16)
    rest = value - first.astype(F32)
    second = rest.astype(BF16)
    third = (rest - second.astype(F32)).astype(BF16)
    return first.astype(F32), second.astype(F32), third.astype(F32)


def kernel(
    dose, labs, live, weights, out,
    own, surplus, surplus_lab, own_lab, cols,
    rows, row_labs, sums, far_sums, panel, turned,
    partial, far_partial, folded, far_folded,
    own_sem, sur_send, sur_recv, slice_send, slice_recv, lab_send, lab_recv,
    sum_send, sum_recv, ring_send, ring_recv, core_send, core_recv,
    z_send, z_recv, part_send, part_recv, fold_send, fold_recv,
):
    y, xl, core, z, xh = (lax.axis_index(a) for a in ("y", "xl", "co", "z", "xh"))
    x = 2 * xh + xl

    def plus(i, d, n):
        return lax.rem(i + d, n)

    def at_x(i, c):
        return {"xh": lax.div(i, 2), "xl": lax.rem(i, 2), "co": c}

    def remote(src, dst, send, recv, device):
        return pltpu.make_async_remote_copy(
            src_ref=src, dst_ref=dst, send_sem=send, recv_sem=recv,
            device_id=device, device_id_type=MESH,
        )

    take_own = pltpu.make_async_copy(dose.at[pl.ds(0, ROWS)], own, own_sem)
    take_own.start()

    barrier = pltpu.get_barrier_semaphore()
    peers = [{"y": plus(y, d, 4)} for d in (1, 2, 3)]
    peers += [{"z": plus(z, d, 8)} for d in (1, 7)]
    peers += [
        at_x(plus(x, d, 4), plus(core, c, 2))
        for d in range(4) for c in range(2) if d or c
    ]
    for peer in peers:
        pl.semaphore_signal(barrier, inc=1, device_id=peer, device_id_type=MESH)
    pl.semaphore_wait(barrier, len(peers))

    opposite = {"y": plus(y, 2, 4)}
    sends = [
        remote(labs.at[1], surplus_lab, sur_send.at[3], sur_recv.at[3], opposite)
    ]
    for b in range(3):
        sends.append(remote(
            dose.at[pl.ds(ROWS + b * BLOCK, BLOCK)], surplus.at[pl.ds(b * BLOCK, BLOCK)],
            sur_send.at[b], sur_recv.at[b], opposite,
        ))
    for copy in sends:
        copy.start()
    take_own.wait()
    count = live[0]
    for copy in sends:
        copy.wait()
    own_lab[...] = jnp.maximum(labs[0], surplus_lab[...])
    for slot in range(HALF):
        block = own[slot * BLOCK : (slot + 1) * BLOCK, :]
        if slot:
            at = (3 - slot) * BLOCK
            other = surplus[at : at + BLOCK, :]
            block = jnp.where(slot < count, block, other)
        for s in range(4):
            cols[s, slot * BLOCK : (slot + 1) * BLOCK, :] = block[:, s * LANES : (s + 1) * LANES]

    mine = 2 * xl + core
    for d in range(4):
        target = plus(x, d, 4)
        device = at_x(target, xh)
        src, dst = cols.at[target], rows.at[mine]
        lab_dst = row_labs.at[mine]
        if d:
            remote(src, dst, slice_send.at[d], slice_recv.at[mine], device).start()
            remote(own_lab, lab_dst, lab_send.at[d], lab_recv.at[mine], device).start()
        else:
            @pl.when(xh != core)
            def _():
                remote(src, dst, slice_send.at[0], slice_recv.at[mine], device).start()
                remote(own_lab, lab_dst, lab_send.at[0], lab_recv.at[mine], device).start()

            @pl.when(xh == core)
            def _():
                pltpu.make_async_copy(src, dst, slice_recv.at[mine]).start()
                pltpu.make_async_copy(own_lab, lab_dst, lab_recv.at[mine]).start()

    cohorts = lax.broadcasted_iota(jnp.int32, (COHORTS, ROWS), 0).astype(F32)

    def one_hot(slot):
        return jnp.where(row_labs[slot] == cohorts, 1.0, 0.0).astype(F32)

    def stacked(hot):
        return jnp.concatenate([hot, hot, hot, jnp.zeros_like(hot)], axis=0).astype(BF16)

    for slot in range(4):
        pltpu.make_async_copy(cols.at[0], rows.at[slot], slice_recv.at[slot]).wait()
        pltpu.make_async_copy(own_lab, row_labs.at[slot], lab_recv.at[slot]).wait()

    total = jnp.zeros((24, LANES), F32)
    for slot in range(4):
        hot = one_hot(slot)
        hots = stacked(hot)
        value = rows[slot]
        wide = value.astype(F32)
        square = wide * wide
        high = square.astype(BF16)
        low = (square - high.astype(F32)).astype(BF16)
        dots = [jnp.dot(hots, v, preferred_element_type=F32)[:COHORTS] for v in (value, high, low)]
        members = jnp.broadcast_to(jnp.sum(hot, axis=1, keepdims=True), (COHORTS, LANES))
        total = total + jnp.concatenate([dots[0], dots[1] + dots[2], members], axis=0)
    sums[...] = total
    sends = [
        remote(sums, far_sums.at[d - 1], sum_send.at[d - 1], sum_recv.at[d - 1], {"y": plus(y, d, 4)})
        for d in (1, 2, 3)
    ]
    for copy in sends:
        copy.start()
    for copy in sends:
        copy.wait()
    total = sums[...] + far_sums[0] + far_sums[1] + far_sums[2]
    size = total[16:24]
    mean = total[0:8] / size
    var = total[8:16] / size - mean * mean + EPSILON
    spread = lax.rsqrt(var)
    spread = spread * (1.5 - 0.5 * var * spread * spread)
    weight = jnp.zeros((COHORTS, LANES), F32)
    all_weights = jnp.float32(0.0)
    labels = lax.broadcasted_iota(jnp.int32, (COHORTS, LANES), 0)
    for c in range(COHORTS):
        w = weights[c].astype(F32)
        all_weights = all_weights + w
        weight = jnp.where(labels == c, w, weight)
    multiplier = spread * jnp.sqrt(weight / all_weights / size)
    table = jnp.concatenate([
        jnp.concatenate(list(split_three(mean)) + [jnp.zeros_like(mean)], axis=0),
        jnp.concatenate(list(split_three(multiplier)) + [jnp.zeros_like(mean)], axis=0),
    ], axis=1).astype(BF16)

    group = 4 * core + x

    def lanes(g):
        return pl.ds(pl.multiple_of(g * LANES, LANES), LANES)

    for slot in range(4):
        hots = stacked(one_hot(slot))
        found = lax.dot_general(hots, table, (((0,), (0,)), ((), ())), preferred_element_type=F32)
        scaled = (rows[slot].astype(F32) - found[:, :LANES]) * found[:, LANES:]
        panel[slot * ROWS : (slot + 1) * ROWS, lanes(group)] = scaled.astype(BF16)
        turned[z, :, slot * ROWS : (slot + 1) * ROWS] = scaled.T.astype(BF16)

    half_lanes = LANES // 2

    def z_copy(step, way):
        d = (9 - step) if way == 0 else (step - 1)
        src = plus(z, d, 8)
        ref = turned.at[src]
        if step == 4:
            ref = turned.at[src, pl.ds(way * half_lanes, half_lanes)]
        return remote(
            ref, ref, z_send.at[way, step - 1], z_recv.at[way, step - 1],
            {"z": plus(z, 1 if way == 0 else 7, 8)},
        )

    def z_wait_recv(step, way):
        z_copy(step, way).wait_recv()

    def ring_copy(which):
        right, left = plus(x, 1, 4), plus(x, 3, 4)
        who = (x, x, left, right)[which]
        ref = panel.at[:, lanes(4 * core + who)]
        if which >= 2:
            half = pl.ds((which - 2) * (DEPTH // 2), DEPTH // 2)
            ref = panel.at[half, lanes(4 * core + who)]
        return remote(
            ref, ref, ring_send.at[which], ring_recv.at[which],
            at_x((right, left, right, left)[which], core),
        )

    def core_copy(d):
        ref = panel.at[:, lanes(4 * core + plus(x, d, 4))]
        return remote(ref, ref, core_send.at[d], core_recv.at[d], {"co": 1 - core})

    z_copy(1, 0).start()
    z_copy(1, 1).start()
    ring_copy(0).start()
    ring_copy(1).start()
    core_copy(0).start()
    ring_copy(0).wait_recv()
    ring_copy(2).start()
    core_copy(3).start()
    ring_copy(1).wait_recv()
    ring_copy(3).start()
    core_copy(1).start()
    z_wait_recv(1, 0)
    z_copy(2, 0).start()
    z_wait_recv(1, 1)
    z_copy(2, 1).start()
    ring_copy(2).wait_recv()
    ring_copy(3).wait_recv()
    core_copy(2).start()
    for d in range(4):
        core_copy(d).wait_recv()

    def part_copy(s):
        owner = lax.div(s, 2)
        slot = lax.rem(y - owner + 3, 4)
        return remote(
            partial.at[s], far_partial.at[slot, lax.rem(s, 2)],
            part_send.at[s], part_recv.at[slot, lax.rem(s, 2)], {"y": owner},
        )

    def make_partial(s):
        left = turned[s]

        def tile(n, carry):
            at = pl.ds(pl.multiple_of(n * 256, 256), 256)
            partial[s, :, at] = jnp.dot(left, panel[:, at], preferred_element_type=F32).astype(BF16)
            return carry

        lax.fori_loop(0, 4, tile, 0)

        @pl.when(lax.div(s, 2) != y)
        def _():
            part_copy(s).start()

    make_partial(z)
    make_partial(plus(z, 7, 8))
    make_partial(plus(z, 1, 8))
    for step in (2, 3, 4):
        for way in (0, 1):
            z_wait_recv(step, way)
            if step < 4:
                z_copy(step + 1, way).start()
        if step < 4:
            make_partial(plus(z, 8 - step, 8))
            make_partial(plus(z, step, 8))
        else:
            make_partial(plus(z, 4, 8))

    def fold_copy(d):
        target = plus(x, d, 4)
        src = folded.at[lax.rem(target, 2), :, pl.ds(pl.multiple_of(lax.div(target, 2) * PANEL, PANEL), PANEL)]
        return remote(src, far_folded.at[d - 1], fold_send.at[d - 1], fold_recv.at[d - 1], at_x(target, core))

    for half in range(2):
        for slot in range(3):
            pltpu.make_async_copy(partial.at[0], far_partial.at[slot, half], part_recv.at[slot, half]).wait()
        added = partial[2 * y + half].astype(F32)
        for slot in range(3):
            added = added + far_partial[slot, half].astype(F32)
        folded[half] = added.astype(BF16)
    for d in (1, 2, 3):
        fold_copy(d).start()

    def put(source, value):
        out[pl.ds(pl.multiple_of(source * LANES, LANES), LANES), :] = value.astype(F32)

    put(x, folded[xl, :, pl.ds(pl.multiple_of(xh * PANEL, PANEL), PANEL)])
    for d in (1, 2, 3):
        fold_copy(d).wait_recv()
        put(plus(x, 4 - d, 4), far_folded[d - 1])

    for d in range(4):
        if d:
            remote(cols.at[0], rows.at[mine], slice_send.at[d], slice_recv.at[mine], at_x(x, core)).wait_send()
            remote(own_lab, row_labs.at[mine], lab_send.at[d], lab_recv.at[mine], at_x(x, core)).wait_send()
        else:
            @pl.when(xh != core)
            def _():
                remote(cols.at[0], rows.at[mine], slice_send.at[0], slice_recv.at[mine], at_x(x, core)).wait_send()
                remote(own_lab, row_labs.at[mine], lab_send.at[0], lab_recv.at[mine], at_x(x, core)).wait_send()
    for d in range(4):
        ring_copy(d).wait_send()
        core_copy(d).wait_send()
        for way in (0, 1):
            z_copy(d + 1, way).wait_send()
    for s in range(8):
        @pl.when(y != s // 2)
        def _():
            part_copy(jnp.int32(s)).wait_send()
    for d in (1, 2, 3):
        fold_copy(d).wait_send()


def shards(dosage, cohort, live_blocks, weight_counts):
    slot = lax.broadcasted_iota(jnp.int32, cohort.shape, 0) // BLOCK
    code = jnp.where(slot < live_blocks[0], cohort, -1).astype(F32).reshape(7, BLOCK)
    none = jnp.full((BLOCK,), -1.0, F32)
    labs = jnp.stack([
        jnp.concatenate([code[0], code[1], code[2], code[3]]),
        jnp.concatenate([none, code[6], code[5], code[4]]),
    ])
    labs = jnp.broadcast_to(labs[:, None, :], (2, COHORTS, ROWS))
    vmem = pl.BlockSpec(memory_space=pltpu.VMEM)
    smem = pl.BlockSpec(memory_space=pltpu.SMEM)
    dma = pltpu.SemaphoreType.DMA
    return pl.pallas_call(
        kernel,
        out_shape=jax.ShapeDtypeStruct((PANEL, PANEL), F32),
        in_specs=[pl.BlockSpec(memory_space=pl.ANY), vmem, smem, smem],
        out_specs=vmem,
        scratch_shapes=[
            pltpu.VMEM((ROWS, PANEL), BF16),
            pltpu.VMEM((SURPLUS, PANEL), BF16),
            pltpu.VMEM((COHORTS, ROWS), F32),
            pltpu.VMEM((COHORTS, ROWS), F32),
            pltpu.VMEM((4, ROWS, LANES), BF16),
            pltpu.VMEM((4, ROWS, LANES), BF16),
            pltpu.VMEM((4, COHORTS, ROWS), F32),
            pltpu.VMEM((24, LANES), F32),
            pltpu.VMEM((3, 24, LANES), F32),
            pltpu.VMEM((DEPTH, 8 * LANES), BF16),
            pltpu.VMEM((8, LANES, DEPTH), BF16),
            pltpu.VMEM((8, LANES, 8 * LANES), BF16),
            pltpu.VMEM((3, 2, LANES, 8 * LANES), BF16),
            pltpu.VMEM((2, LANES, 8 * LANES), BF16),
            pltpu.VMEM((3, LANES, PANEL), BF16),
            dma, dma((4,)), dma((4,)), dma((4,)), dma((4,)), dma((4,)), dma((4,)),
            dma((3,)), dma((3,)), dma((4,)), dma((4,)), dma((4,)), dma((4,)),
            dma((2, 4)), dma((2, 4)), dma((8,)), dma((3, 2)), dma((3,)), dma((3,)),
        ],
        compiler_params=pltpu.CompilerParams(
            collective_id=0, has_side_effects=True, vmem_limit_bytes=60 * 1024 * 1024
        ),
    )(dosage, labs, live_blocks, weight_counts)


def solution(mesh):
    torus = Mesh(mesh.devices.reshape(4, 2, 2, 8, 2), ("y", "xl", "co", "z", "xh"))
    samp, var = ("y", "xl", "co"), ("z", "xh")
    placed = (P(samp, var), P(samp), P(samp), P())
    return jax.shard_map(
        shards, mesh=torus, in_specs=placed, out_specs=P(samp, var), check_vma=False
    )
```

```python
import jax
import jax.numpy as jnp
from jax import lax
from jax.experimental import pallas as pl
from jax.experimental.pallas import tpu as pltpu
from jax.sharding import Mesh
from jax.sharding import PartitionSpec as P

COHORTS = 8
BLOCK = 96
HALF = 4
ROWS = HALF * BLOCK
LANES = 128
PANEL = 512
DEPTH = 4 * ROWS
WIDTH = 2 * PANEL
EPSILON = 1e-05
MESH = pl.DeviceIdType.MESH
F32 = jnp.float32
BF16 = jnp.bfloat16


def split_three(value):
    first = value.astype(BF16)
    rest = value - first.astype(F32)
    second = rest.astype(BF16)
    third = (rest - second.astype(F32)).astype(BF16)
    return first.astype(F32), second.astype(F32), third.astype(F32)


def kernel(
    dose, labs, live, weights, out,
    own, relay, surplus, surplus_lab, own_lab, cols,
    raw, row_labs, hot_ref, sums, far_sums, row_tab, z_tab,
    z_raw, panel, turned, keep, partial, mid_in, acc_in, dir_in, folded,
    own_sem, sur_send, sur_recv, rel_send, rel_recv, surlab_send, surlab_recv,
    slice_send, slice_recv, lab_send, lab_recv, sum_send, sum_recv,
    rowtab_send, rowtab_recv, ztab_send, ztab_recv,
    ring_send, ring_recv, fwd_send, fwd_recv, core_send, core_recv,
    z_send, z_recv, part_send, mid_recv, acc_recv, dir_recv, fold_send, fold_recv,
):
    y, xl, core, z, xh = (lax.axis_index(a) for a in ("y", "xl", "co", "z", "xh"))
    x = 2 * xh + xl

    def plus(i, d, n):
        return lax.rem(i + d, n)

    def at_x(i, c):
        return {"xh": lax.div(i, 2), "xl": lax.rem(i, 2), "co": c}

    def remote(src, dst, send, recv, device):
        return pltpu.make_async_remote_copy(
            src_ref=src, dst_ref=dst, send_sem=send, recv_sem=recv,
            device_id=device, device_id_type=MESH,
        )

    take_own = pltpu.make_async_copy(dose.at[pl.ds(0, ROWS)], own, own_sem)
    take_own.start()

    barrier = pltpu.get_barrier_semaphore()
    row_peers = [(d, c) for d in range(4) for c in range(2) if d or c]
    peers = [{"y": plus(y, d, 4)} for d in (1, 2, 3)]
    peers += [{"z": plus(z, d, 8)} for d in range(1, 8)]
    peers += [at_x(plus(x, d, 4), plus(core, c, 2)) for d, c in row_peers]
    for peer in peers:
        pl.semaphore_signal(barrier, inc=1, device_id=peer, device_id_type=MESH)
    pl.semaphore_wait(barrier, len(peers))

    drains = []

    onward = {"y": plus(y, 1 + 2 * core, 4)}
    opposite = {"y": plus(y, 2, 4)}

    def sur_copy(b):
        return remote(
            dose.at[pl.ds((6 - b) * BLOCK, BLOCK)], relay.at[b], sur_send.at[b], sur_recv.at[b], onward
        )

    def rel_copy(b):
        return remote(relay.at[b], surplus.at[b], rel_send.at[b], rel_recv.at[b], onward)

    surlab_copy = remote(labs.at[1], surplus_lab, surlab_send, surlab_recv, opposite)
    for b in range(3):
        sur_copy(b).start()
        drains.append(sur_copy(b))
        drains.append(rel_copy(b))
    surlab_copy.start()
    drains.append(surlab_copy)

    def pass_relay(b):
        sur_copy(b).wait_recv()
        rel_copy(b).start()

    group = 4 * core + x
    mine = 2 * xl + core

    def band(slot):
        return pl.ds(slot * BLOCK, BLOCK)

    def slice_copy(slot, d):
        target = plus(x, d, 4)
        if slot == 0:
            src = own.at[band(0), pl.ds(pl.multiple_of(target * LANES, LANES), LANES)]
        else:
            src = cols.at[target, band(slot)]
        dst = raw.at[4 * xh + target, mine, band(slot)]
        return remote(src, dst, slice_send.at[slot, d], slice_recv.at[slot, mine], at_x(target, xh))

    def slice_local(slot):
        if slot == 0:
            src = own.at[band(0), pl.ds(pl.multiple_of(x * LANES, LANES), LANES)]
        else:
            src = cols.at[x, band(slot)]
        return pltpu.make_async_copy(src, raw.at[group, mine, band(slot)], slice_recv.at[slot, mine])

    def lab_copy(d):
        target = plus(x, d, 4)
        return remote(
            own_lab, row_labs.at[mine], lab_send.at[d], lab_recv.at[mine], at_x(target, xh)
        )

    def send_slices(slot):
        for d in (1, 2, 3):
            slice_copy(slot, d).start()
            drains.append(slice_copy(slot, d))

        @pl.when(xh != core)
        def _():
            slice_copy(slot, 0).start()

        @pl.when(xh == core)
        def _():
            slice_local(slot).start()

    def send_labels():
        surlab_copy.wait_recv()
        own_lab[...] = jnp.maximum(labs[0], surplus_lab[...])
        for d in (1, 2, 3):
            lab_copy(d).start()
            drains.append(lab_copy(d))

        @pl.when(xh != core)
        def _():
            lab_copy(0).start()

        @pl.when(xh == core)
        def _():
            pltpu.make_async_copy(own_lab, row_labs.at[mine], lab_recv.at[mine]).start()

    def fill_slot(slot):
        rel_copy(slot - 1).wait_recv()
        block = jnp.where(slot < live[0], own[slot * BLOCK : (slot + 1) * BLOCK, :], surplus[slot - 1])
        for s in range(4):
            cols[s, slot * BLOCK : (slot + 1) * BLOCK, :] = block[:, s * LANES : (s + 1) * LANES]
        send_slices(slot)

    def z_copy(step, way, slot):
        d = (9 - step) if way == 0 else (step - 1)
        at = plus(z, d, 8)
        dst = z_raw.at[at, :, band(slot)]
        src = raw.at[group, :, band(slot)] if step == 1 else dst
        return remote(
            src, dst, z_send.at[way, step - 1, slot], z_recv.at[way, step - 1, slot],
            {"z": plus(z, 1 if way == 0 else 7, 8)},
        )

    def goes(step, way, slot):
        return step < 4 or (slot < 2) == (way == 0)

    def z_start(step, way, slot):
        if goes(step, way, slot):
            z_copy(step, way, slot).start()
            drains.append(z_copy(step, way, slot))

    def z_pass(step, slot):
        for way in (0, 1):
            if goes(step, way, slot):
                z_copy(step, way, slot).wait_recv()
                if step < 4:
                    z_start(step + 1, way, slot)

    right, left = plus(x, 1, 4), plus(x, 3, 4)

    def ring_copy(way, slot):
        ref = raw.at[group, :, band(slot)]
        return remote(
            ref, ref, ring_send.at[way, slot], ring_recv.at[way, slot],
            at_x(right if way == 0 else left, core),
        )

    def fwd_copy(slot):
        who, to = (left, right) if slot < 2 else (right, left)
        ref = raw.at[4 * core + who, :, band(slot)]
        return remote(ref, ref, fwd_send.at[slot], fwd_recv.at[slot], at_x(to, core))

    def core_copy(d, slot):
        ref = raw.at[4 * core + plus(x, d, 4), :, band(slot)]
        return remote(ref, ref, core_send.at[d, slot], core_recv.at[d, slot], {"co": 1 - core})

    def core_start(d, slot):
        core_copy(d, slot).start()
        drains.append(core_copy(d, slot))

    def send_slot(slot):
        for source in range(4):
            pltpu.make_async_copy(
                cols.at[0, band(slot)], raw.at[group, source, band(slot)], slice_recv.at[slot, source]
            ).wait()
        for way in (0, 1):
            z_start(1, way, slot)
        for way in (0, 1):
            ring_copy(way, slot).start()
            drains.append(ring_copy(way, slot))
        core_start(0, slot)

    def pass_ring(slot):
        ring_copy(0, slot).wait_recv()
        if slot < 2:
            fwd_copy(slot).start()
        core_start(3, slot)
        ring_copy(1, slot).wait_recv()
        if slot >= 2:
            fwd_copy(slot).start()
        core_start(1, slot)
        drains.append(fwd_copy(slot))

    def pass_far(slot):
        fwd_copy(slot).wait_recv()
        core_start(2, slot)

    take_own.wait()
    send_slices(0)
    send_labels()
    pass_relay(0)
    send_slot(0)
    pass_relay(1)
    fill_slot(1)
    pass_relay(2)
    z_pass(1, 0)
    pass_ring(0)
    fill_slot(2)
    send_slot(1)
    fill_slot(3)
    send_slot(2)
    z_pass(2, 0)
    z_pass(1, 1)
    pass_ring(1)
    pass_far(0)
    send_slot(3)

    for source in range(4):
        pltpu.make_async_copy(own_lab, row_labs.at[source], lab_recv.at[source]).wait()
    cohorts = lax.broadcasted_iota(jnp.int32, (COHORTS, ROWS), 0).astype(F32)
    total = jnp.zeros((24, LANES), F32)
    for source in range(4):
        hot = jnp.where(row_labs[source] == cohorts, 1.0, 0.0).astype(F32)
        hots = jnp.concatenate([hot, hot, hot, jnp.zeros_like(hot)], axis=0).astype(BF16)
        hot_ref[source] = hots
        value = raw[group, source]
        wide = value.astype(F32)
        square = wide * wide
        high = square.astype(BF16)
        low = (square - high.astype(F32)).astype(BF16)
        dots = [jnp.dot(hots, v, preferred_element_type=F32)[:COHORTS] for v in (value, high, low)]
        members = jnp.broadcast_to(jnp.sum(hot, axis=1, keepdims=True), (COHORTS, LANES))
        total = total + jnp.concatenate([dots[0], dots[1] + dots[2], members], axis=0)
    sums[...] = total
    sum_copies = [
        remote(sums, far_sums.at[d - 1], sum_send.at[d - 1], sum_recv.at[d - 1], {"y": plus(y, d, 4)})
        for d in (1, 2, 3)
    ]
    for copy in sum_copies:
        copy.start()
        drains.append(copy)

    z_pass(1, 2)
    pass_ring(2)
    pass_far(1)

    for copy in sum_copies:
        copy.wait_recv()
    total = sums[...] + far_sums[0] + far_sums[1] + far_sums[2]
    size = total[16:24]
    mean = total[0:8] / size
    var = total[8:16] / size - mean * mean + EPSILON
    spread = lax.rsqrt(var)
    spread = spread * (1.5 - 0.5 * var * spread * spread)
    weight = jnp.zeros((COHORTS, LANES), F32)
    all_weights = jnp.float32(0.0)
    labels = lax.broadcasted_iota(jnp.int32, (COHORTS, LANES), 0)
    for c in range(COHORTS):
        w = weights[c].astype(F32)
        all_weights = all_weights + w
        weight = jnp.where(labels == c, w, weight)
    multiplier = spread * jnp.sqrt(weight / all_weights / size)
    row_tab[group] = jnp.concatenate([mean, multiplier], axis=0)

    def rowtab_copy(d, c):
        ref = row_tab.at[group]
        return remote(
            ref, ref, rowtab_send.at[2 * d + c], rowtab_recv.at[2 * d + c],
            at_x(plus(x, d, 4), plus(core, c, 2)),
        )

    def ztab_copy(d):
        return remote(
            row_tab.at[group], z_tab.at[z], ztab_send.at[d - 1], ztab_recv.at[d - 1], {"z": plus(z, d, 8)}
        )

    for d, c in row_peers:
        rowtab_copy(d, c).start()
        drains.append(rowtab_copy(d, c))
    for d in (1, 7, 2, 6, 3, 5, 4):
        ztab_copy(d).start()
        drains.append(ztab_copy(d))

    z_pass(2, 1)
    z_pass(1, 3)
    pass_ring(3)
    for slot in (2, 3):
        pass_far(slot)
    z_pass(3, 0)

    def packed(both):
        mean, multiplier = both[:COHORTS], both[COHORTS:]
        none = jnp.zeros_like(mean)
        return jnp.concatenate([
            jnp.concatenate(list(split_three(mean)) + [none], axis=0),
            jnp.concatenate(list(split_three(multiplier)) + [none], axis=0),
        ], axis=1).astype(BF16)

    def scaled(value, source, table):
        found = lax.dot_general(
            hot_ref[source], table, (((0,), (0,)), ((), ())), preferred_element_type=F32
        )
        return (value.astype(F32) - found[:, :LANES]) * found[:, LANES:]

    for d, c in row_peers:
        rowtab_copy(d, c).wait_recv()
    for d in range(4):
        for slot in range(4):
            core_copy(d, slot).wait_recv()
    z_pass(2, 2)

    def fill_panel(g, carry):
        table = packed(row_tab[g])
        at = pl.ds(pl.multiple_of(g * LANES, LANES), LANES)
        for source in range(4):
            value = scaled(raw[g, source], source, table)
            panel[source * ROWS : (source + 1) * ROWS, at] = value.astype(BF16)
        return carry

    lax.fori_loop(0, 8, fill_panel, 0)

    sign = 1 - 2 * core

    def hops_to(s):
        return lax.rem(sign * (lax.div(s, 2) - y) + 4, 4)

    def half_of(ref, h):
        return ref.at[:, pl.ds(h * PANEL, PANEL)]

    def part_copy(s, h, kind):
        p = lax.rem(s, 2)
        dst, recv, device = {
            "mid": (mid_in.at[p, h], mid_recv.at[p, h], onward),
            "acc": (acc_in.at[p, h], acc_recv.at[p, h], onward),
            "dir": (dir_in.at[p, h], dir_recv.at[p, h], {"y": plus(y, 3 - 2 * core, 4)}),
        }[kind]
        return remote(half_of(partial.at[s], h), dst, part_send.at[s, h], recv, device)

    def make_partial(s, value_of, table):
        table = packed(table)
        for source in range(4):
            value = scaled(value_of(source), source, table)
            turned[:, source * ROWS : (source + 1) * ROWS] = value.T.astype(BF16)
        hops = hops_to(s)
        for h in range(2):
            def tile(n, carry):
                at = pl.ds(pl.multiple_of(h * PANEL + n * 256, 256), 256)
                value = jnp.dot(turned[...], panel[:, at], preferred_element_type=F32)
                keep[s, :, at] = value
                partial[s, :, at] = value.astype(BF16)
                return carry

            lax.fori_loop(0, 2, tile, 0)

            @pl.when(hops == 2)
            def _():
                part_copy(s, h, "mid").start()

            @pl.when(hops == 3)
            def _():
                part_copy(s, h, "dir").start()

    def add_relay(s):
        @pl.when(hops_to(s) == 1)
        def _():
            for h in range(2):
                p = lax.rem(s, 2)
                part_copy(s, h, "mid").wait_recv()
                at = slice(h * PANEL, (h + 1) * PANEL)
                partial[s, :, at] = (keep[s, :, at] + mid_in[p, h].astype(F32)).astype(BF16)
                part_copy(s, h, "acc").start()

    def from_z(d):
        s = plus(z, d, 8)
        ztab_copy(8 - d).wait_recv()
        make_partial(s, lambda source: z_raw[s, source], z_tab[s])

    make_partial(z, lambda source: raw[group, source], row_tab[group])
    z_pass(2, 3)
    z_pass(3, 1)
    from_z(7)
    from_z(1)
    add_relay(z)
    z_pass(3, 2)
    z_pass(3, 3)
    from_z(6)
    add_relay(plus(z, 7, 8))
    from_z(2)
    add_relay(plus(z, 1, 8))
    from_z(5)
    add_relay(plus(z, 6, 8))
    from_z(3)
    add_relay(plus(z, 2, 8))
    add_relay(plus(z, 5, 8))
    for slot in range(4):
        z_pass(4, slot)
    from_z(4)
    add_relay(plus(z, 3, 8))
    add_relay(plus(z, 4, 8))

    def fold_copy(p, h):
        target = 2 * h + p
        d = plus(target, 4 - x, 4) - 1
        return remote(
            folded.at[p, h], out.at[pl.ds(pl.multiple_of(x * LANES, LANES), LANES)],
            fold_send.at[p, h], fold_recv.at[d], at_x(target, core),
        )

    for p in (plus(z, 1, 2), plus(z, 0, 2)):
        for h in range(2):
            s = 2 * y + p
            part_copy(s, h, "acc").wait_recv()
            part_copy(s, h, "dir").wait_recv()
            at = slice(h * PANEL, (h + 1) * PANEL)
            value = keep[s, :, at] + acc_in[p, h].astype(F32) + dir_in[p, h].astype(F32)
            value = value.astype(BF16)

            @pl.when(2 * h + p != x)
            def _():
                folded[p, h] = value
                fold_copy(p, h).start()

            @pl.when(2 * h + p == x)
            def _():
                out[pl.ds(pl.multiple_of(x * LANES, LANES), LANES), :] = value

    for d in (1, 2, 3):
        pltpu.make_async_copy(
            folded.at[0, 0], out.at[pl.ds(0, LANES)], fold_recv.at[d - 1]
        ).wait()

    for copy in drains:
        copy.wait_send()

    @pl.when(xh != core)
    def _():
        for slot in range(4):
            slice_copy(slot, 0).wait_send()
        lab_copy(0).wait_send()

    for s in range(8):
        @pl.when(y != s // 2)
        def _():
            for h in range(2):
                part_copy(jnp.int32(s), h, "dir").wait_send()

    for p in range(2):
        for h in range(2):
            @pl.when(2 * h + p != x)
            def _():
                fold_copy(p, h).wait_send()


def shards(dosage, cohort, live_blocks, weight_counts):
    slot = lax.broadcasted_iota(jnp.int32, cohort.shape, 0) // BLOCK
    code = jnp.where(slot < live_blocks[0], cohort, -1).astype(F32).reshape(7, BLOCK)
    none = jnp.full((BLOCK,), -1.0, F32)
    labs = jnp.stack([
        jnp.concatenate([code[0], code[1], code[2], code[3]]),
        jnp.concatenate([none, code[6], code[5], code[4]]),
    ])
    labs = jnp.broadcast_to(labs[:, None, :], (2, COHORTS, ROWS))
    vmem = pl.BlockSpec(memory_space=pltpu.VMEM)
    smem = pl.BlockSpec(memory_space=pltpu.SMEM)

    def dma(*shape):
        return pltpu.SemaphoreType.DMA(shape)

    ld = pl.pallas_call(
        kernel,
        out_shape=jax.ShapeDtypeStruct((PANEL, PANEL), BF16),
        in_specs=[pl.BlockSpec(memory_space=pl.ANY), vmem, smem, smem],
        out_specs=vmem,
        scratch_shapes=[
            pltpu.VMEM((ROWS, PANEL), BF16),
            pltpu.VMEM((3, BLOCK, PANEL), BF16),
            pltpu.VMEM((3, BLOCK, PANEL), BF16),
            pltpu.VMEM((COHORTS, ROWS), F32),
            pltpu.VMEM((COHORTS, ROWS), F32),
            pltpu.VMEM((4, ROWS, LANES), BF16),
            pltpu.VMEM((8, 4, ROWS, LANES), BF16),
            pltpu.VMEM((4, COHORTS, ROWS), F32),
            pltpu.VMEM((4, 32, ROWS), BF16),
            pltpu.VMEM((24, LANES), F32),
            pltpu.VMEM((3, 24, LANES), F32),
            pltpu.VMEM((8, 16, LANES), F32),
            pltpu.VMEM((8, 16, LANES), F32),
            pltpu.VMEM((8, 4, ROWS, LANES), BF16),
            pltpu.VMEM((DEPTH, WIDTH), BF16),
            pltpu.VMEM((LANES, DEPTH), BF16),
            pltpu.VMEM((8, LANES, WIDTH), F32),
            pltpu.VMEM((8, LANES, WIDTH), BF16),
            pltpu.VMEM((2, 2, LANES, PANEL), BF16),
            pltpu.VMEM((2, 2, LANES, PANEL), BF16),
            pltpu.VMEM((2, 2, LANES, PANEL), BF16),
            pltpu.VMEM((2, 2, LANES, PANEL), BF16),
            pltpu.SemaphoreType.DMA, dma(3), dma(3), dma(3), dma(3),
            pltpu.SemaphoreType.DMA, pltpu.SemaphoreType.DMA,
            dma(4, 4), dma(4, 4), dma(4), dma(4), dma(3), dma(3),
            dma(8), dma(8), dma(7), dma(7),
            dma(2, 4), dma(2, 4), dma(4), dma(4), dma(4, 4), dma(4, 4),
            dma(2, 4, 4), dma(2, 4, 4), dma(8, 2), dma(2, 2), dma(2, 2), dma(2, 2),
            dma(2, 2), dma(3),
        ],
        compiler_params=pltpu.CompilerParams(
            collective_id=0, has_side_effects=True, vmem_limit_bytes=60 * 1024 * 1024
        ),
    )(dosage, labs, live_blocks, weight_counts)
    return ld.astype(F32)


def solution(mesh):
    torus = Mesh(mesh.devices.reshape(4, 2, 2, 8, 2), ("y", "xl", "co", "z", "xh"))
    samp, var = ("y", "xl", "co"), ("z", "xh")
    placed = (P(samp, var), P(samp), P(samp), P())
    return jax.shard_map(
        shards, mesh=torus, in_specs=placed, out_specs=P(samp, var), check_vma=False
    )
```

```python
import jax
import jax.numpy as jnp
from jax import lax
from jax.experimental import pallas as pl
from jax.experimental.pallas import tpu as pltpu
from jax.sharding import Mesh
from jax.sharding import PartitionSpec as P

COHORTS = 8
BLOCK = 96
HALF = 4
SURPLUS = 3 * BLOCK
ROWS = HALF * BLOCK
LANES = 128
PANEL = 512
DEPTH = 4 * ROWS
WIDTH = 2 * PANEL
EPSILON = 1e-05
MESH = pl.DeviceIdType.MESH
F32 = jnp.float32
BF16 = jnp.bfloat16


def split_three(value):
    first = value.astype(BF16)
    rest = value - first.astype(F32)
    second = rest.astype(BF16)
    third = (rest - second.astype(F32)).astype(BF16)
    return first.astype(F32), second.astype(F32), third.astype(F32)


def kernel(
    dose, labs, live, weights, out,
    own, surplus, surplus_lab, own_lab, cols,
    raw, row_labs, hot_ref, slice_sums, row_sums, sums, far_sums, row_tab, z_tab,
    z_raw, panel, turned, keep, partial, mid_in, acc_in, dir_in, folded,
    own_sem, sur_send, sur_recv, surlab_send, surlab_recv,
    slice_send, slice_recv, lab_send, lab_recv, rowsum_send, rowsum_recv, sum_send, sum_recv,
    rowtab_send, rowtab_recv, ztab_send, ztab_recv,
    ring_send, ring_recv, fwd_send, fwd_recv, core_send, core_recv,
    z_send, z_recv, part_send, mid_recv, acc_recv, dir_recv, fold_send, fold_recv,
):
    y, xl, core, z, xh = (lax.axis_index(a) for a in ("y", "xl", "co", "z", "xh"))
    x = 2 * xh + xl

    def plus(i, d, n):
        return lax.rem(i + d, n)

    def at_x(i, c):
        return {"xh": lax.div(i, 2), "xl": lax.rem(i, 2), "co": c}

    def remote(src, dst, send, recv, device):
        return pltpu.make_async_remote_copy(
            src_ref=src, dst_ref=dst, send_sem=send, recv_sem=recv,
            device_id=device, device_id_type=MESH,
        )

    take_own = pltpu.make_async_copy(dose, own, own_sem)
    take_own.start()

    barrier = pltpu.get_barrier_semaphore()
    row_peers = [(d, c) for d in range(4) for c in range(2) if d or c]
    peers = [{"y": plus(y, d, 4)} for d in (1, 2, 3)]
    peers += [{"z": plus(z, d, 8)} for d in (1, 7)]
    peers += [at_x(plus(x, d, 4), plus(core, c, 2)) for d, c in row_peers]
    for peer in peers:
        pl.semaphore_signal(barrier, inc=1, device_id=peer, device_id_type=MESH)

    take_own.wait()
    cohorts = lax.broadcasted_iota(jnp.int32, (COHORTS, ROWS), 0).astype(F32)
    totals = None
    for first, count, labels in ((0, ROWS, labs[0]), (ROWS, SURPLUS, labs[2])):
        hot = jnp.where(labels == cohorts, 1.0, 0.0).astype(F32)[:, :count]
        hots = jnp.concatenate([hot, hot], axis=0).astype(BF16)
        value = own[first : first + count, :]
        wide = value.astype(F32)
        square = wide * wide
        high = square.astype(BF16)
        low = (square - high.astype(F32)).astype(BF16)
        dots = [jnp.dot(hots, v, preferred_element_type=F32)[:COHORTS] for v in (value, high, low)]
        members = jnp.broadcast_to(jnp.sum(hot, axis=1, keepdims=True), (COHORTS, PANEL))
        part = jnp.concatenate([dots[0], dots[1] + dots[2], members], axis=0)
        totals = part if totals is None else totals + part
    for s in range(4):
        slice_sums[s] = totals[:, s * LANES : (s + 1) * LANES]
    pl.semaphore_wait(barrier, len(peers))

    drains = []

    opposite = {"y": plus(y, 2, 4)}
    onward = {"y": plus(y, 1 + 2 * core, 4)}

    def sur_copy(b):
        return remote(
            dose.at[pl.ds((6 - b) * BLOCK, BLOCK)], surplus.at[b], sur_send.at[b], sur_recv.at[b], opposite
        )

    surlab_copy = remote(labs.at[1], surplus_lab, surlab_send, surlab_recv, opposite)

    def send_surplus():
        for b in range(3):
            sur_copy(b).start()
            drains.append(sur_copy(b))
            if b == 0:
                surlab_copy.start()
                drains.append(surlab_copy)

    group = 4 * core + x
    mine = 2 * xl + core

    def band(slot):
        return pl.ds(slot * BLOCK, BLOCK)

    def slice_copy(slot, d):
        target = plus(x, d, 4)
        if slot == 0:
            src = own.at[band(0), pl.ds(pl.multiple_of(target * LANES, LANES), LANES)]
        else:
            src = cols.at[target, band(slot)]
        dst = raw.at[4 * xh + target, mine, band(slot)]
        return remote(src, dst, slice_send.at[slot, d], slice_recv.at[slot, mine], at_x(target, xh))

    def slice_local(slot):
        if slot == 0:
            src = own.at[band(0), pl.ds(pl.multiple_of(x * LANES, LANES), LANES)]
        else:
            src = cols.at[x, band(slot)]
        return pltpu.make_async_copy(src, raw.at[group, mine, band(slot)], slice_recv.at[slot, mine])

    def lab_copy(d):
        target = plus(x, d, 4)
        return remote(
            own_lab, row_labs.at[mine], lab_send.at[d], lab_recv.at[mine], at_x(target, xh)
        )

    def rowsum_copy(d):
        target = plus(x, d, 4)
        return remote(
            slice_sums.at[target], row_sums.at[mine], rowsum_send.at[d], rowsum_recv.at[mine], at_x(target, xh)
        )

    def send_row_sums():
        for d in (1, 2, 3):
            rowsum_copy(d).start()
            drains.append(rowsum_copy(d))

        @pl.when(xh != core)
        def _():
            rowsum_copy(0).start()

        @pl.when(xh == core)
        def _():
            pltpu.make_async_copy(slice_sums.at[x], row_sums.at[mine], rowsum_recv.at[mine]).start()

    def send_slices(slot):
        for d in (1, 2, 3):
            slice_copy(slot, d).start()
            drains.append(slice_copy(slot, d))

        @pl.when(xh != core)
        def _():
            slice_copy(slot, 0).start()

        @pl.when(xh == core)
        def _():
            slice_local(slot).start()

    def send_labels():
        surlab_copy.wait_recv()
        own_lab[...] = jnp.maximum(labs[0], surplus_lab[...])
        for d in (1, 2, 3):
            lab_copy(d).start()
            drains.append(lab_copy(d))

        @pl.when(xh != core)
        def _():
            lab_copy(0).start()

        @pl.when(xh == core)
        def _():
            pltpu.make_async_copy(own_lab, row_labs.at[mine], lab_recv.at[mine]).start()

    def fill_slot(slot):
        sur_copy(slot - 1).wait_recv()
        block = jnp.where(slot < live[0], own[slot * BLOCK : (slot + 1) * BLOCK, :], surplus[slot - 1])
        for s in range(4):
            cols[s, slot * BLOCK : (slot + 1) * BLOCK, :] = block[:, s * LANES : (s + 1) * LANES]
        send_slices(slot)

    def z_copy(step, way, slot):
        d = (9 - step) if way == 0 else (step - 1)
        at = plus(z, d, 8)
        dst = z_raw.at[at, :, band(slot)]
        src = raw.at[group, :, band(slot)] if step == 1 else dst
        return remote(
            src, dst, z_send.at[way, step - 1, slot], z_recv.at[way, step - 1, slot],
            {"z": plus(z, 1 if way == 0 else 7, 8)},
        )

    def goes(step, way, slot):
        return step < 4 or (slot < 2) == (way == 0)

    def z_start(step, way, slot):
        if goes(step, way, slot):
            z_copy(step, way, slot).start()
            drains.append(z_copy(step, way, slot))

    def z_pass(step, slot):
        for way in (0, 1):
            if goes(step, way, slot):
                z_copy(step, way, slot).wait_recv()
                if step < 4:
                    z_start(step + 1, way, slot)

    right, left = plus(x, 1, 4), plus(x, 3, 4)

    def ring_copy(way, slot):
        ref = raw.at[group, :, band(slot)]
        return remote(
            ref, ref, ring_send.at[way, slot], ring_recv.at[way, slot],
            at_x(right if way == 0 else left, core),
        )

    def fwd_copy(slot):
        who, to = (left, right) if slot < 2 else (right, left)
        ref = raw.at[4 * core + who, :, band(slot)]
        return remote(ref, ref, fwd_send.at[slot], fwd_recv.at[slot], at_x(to, core))

    def core_copy(d, slot):
        ref = raw.at[4 * core + plus(x, d, 4), :, band(slot)]
        return remote(ref, ref, core_send.at[d, slot], core_recv.at[d, slot], {"co": 1 - core})

    def core_start(d, slot):
        core_copy(d, slot).start()
        drains.append(core_copy(d, slot))

    def send_slot(slot):
        for source in range(4):
            pltpu.make_async_copy(
                cols.at[0, band(slot)], raw.at[group, source, band(slot)], slice_recv.at[slot, source]
            ).wait()
        for way in (0, 1):
            z_start(1, way, slot)
        for way in (0, 1):
            ring_copy(way, slot).start()
            drains.append(ring_copy(way, slot))
        core_start(0, slot)

    def pass_ring(slot):
        ring_copy(0, slot).wait_recv()
        if slot < 2:
            fwd_copy(slot).start()
        core_start(3, slot)
        ring_copy(1, slot).wait_recv()
        if slot >= 2:
            fwd_copy(slot).start()
        core_start(1, slot)
        drains.append(fwd_copy(slot))

    def pass_far(slot):
        fwd_copy(slot).wait_recv()
        core_start(2, slot)

    sum_copies = [
        remote(sums, far_sums.at[d - 1], sum_send.at[d - 1], sum_recv.at[d - 1], {"y": plus(y, d, 4)})
        for d in (1, 2, 3)
    ]

    send_slices(0)
    send_row_sums()
    send_surplus()
    for source in range(4):
        pltpu.make_async_copy(slice_sums.at[0], row_sums.at[source], rowsum_recv.at[source]).wait()
    sums[...] = row_sums[0] + row_sums[1] + row_sums[2] + row_sums[3]
    for copy in sum_copies:
        copy.start()
        drains.append(copy)
    send_slot(0)
    send_labels()
    fill_slot(1)

    for copy in sum_copies:
        copy.wait_recv()
    total = sums[...] + far_sums[0] + far_sums[1] + far_sums[2]
    size = total[16:24]
    mean = total[0:8] / size
    var = total[8:16] / size - mean * mean + EPSILON
    spread = lax.rsqrt(var)
    spread = spread * (1.5 - 0.5 * var * spread * spread)
    weight = jnp.zeros((COHORTS, LANES), F32)
    all_weights = jnp.float32(0.0)
    labels = lax.broadcasted_iota(jnp.int32, (COHORTS, LANES), 0)
    for c in range(COHORTS):
        w = weights[c].astype(F32)
        all_weights = all_weights + w
        weight = jnp.where(labels == c, w, weight)
    multiplier = spread * jnp.sqrt(weight / all_weights / size)
    row_tab[group] = jnp.concatenate([mean, multiplier], axis=0)

    def rowtab_copy(d, c):
        ref = row_tab.at[group]
        return remote(
            ref, ref, rowtab_send.at[2 * d + c], rowtab_recv.at[2 * d + c],
            at_x(plus(x, d, 4), plus(core, c, 2)),
        )

    def ztab_copy(step, way):
        at = plus(z, (9 - step) if way == 0 else (step - 1), 8)
        src = row_tab.at[group] if step == 1 else z_tab.at[at]
        return remote(
            src, z_tab.at[at], ztab_send.at[way, step - 1], ztab_recv.at[way, step - 1],
            {"z": plus(z, 1 if way == 0 else 7, 8)},
        )

    def ztab_start(step, way):
        if step < 4 or way == 0:
            ztab_copy(step, way).start()
            drains.append(ztab_copy(step, way))

    def ztab_pass(step):
        for way in (0, 1):
            if step < 4 or way == 0:
                ztab_copy(step, way).wait_recv()
                if step < 4:
                    ztab_start(step + 1, way)

    for d, c in row_peers:
        rowtab_copy(d, c).start()
        drains.append(rowtab_copy(d, c))
    for way in (0, 1):
        ztab_start(1, way)

    pass_ring(0)
    z_pass(1, 0)
    fill_slot(2)
    send_slot(1)
    ztab_pass(1)
    fill_slot(3)
    send_slot(2)
    z_pass(2, 0)
    pass_ring(1)
    z_pass(1, 1)
    pass_far(0)
    send_slot(3)
    for source in range(4):
        pltpu.make_async_copy(own_lab, row_labs.at[source], lab_recv.at[source]).wait()
    for source in range(4):
        hot = jnp.where(row_labs[source] == cohorts, 1.0, 0.0).astype(F32)
        hots = jnp.concatenate([hot, hot, hot, jnp.zeros_like(hot)], axis=0)
        hot_ref[source] = hots.T.astype(BF16)
    ztab_pass(2)
    z_pass(1, 2)
    pass_ring(2)
    pass_far(1)
    z_pass(2, 1)
    z_pass(3, 0)
    z_pass(1, 3)
    pass_ring(3)
    ztab_pass(3)
    for slot in (2, 3):
        pass_far(slot)

    def packed(both):
        mean, multiplier = both[:COHORTS], both[COHORTS:]
        none = jnp.zeros_like(mean)
        return jnp.concatenate([
            jnp.concatenate(list(split_three(mean)) + [none], axis=0),
            jnp.concatenate(list(split_three(multiplier)) + [none], axis=0),
        ], axis=1).astype(BF16)

    def scaled(value, source, table):
        found = jnp.dot(hot_ref[source], table, preferred_element_type=F32)
        return (value.astype(F32) - found[:, :LANES]) * found[:, LANES:]

    for d, c in row_peers:
        rowtab_copy(d, c).wait_recv()
    for d in range(4):
        for slot in range(4):
            core_copy(d, slot).wait_recv()
    z_pass(2, 2)

    def fill_panel(g, carry):
        table = packed(row_tab[g])
        at = pl.ds(pl.multiple_of(g * LANES, LANES), LANES)
        for source in range(4):
            value = scaled(raw[g, source], source, table)
            panel[source * ROWS : (source + 1) * ROWS, at] = value.astype(BF16)
        return carry

    lax.fori_loop(0, 8, fill_panel, 0)

    sign = 1 - 2 * core

    def hops_to(s):
        return lax.rem(sign * (lax.div(s, 2) - y) + 4, 4)

    def half_of(ref, h):
        return ref.at[:, pl.ds(h * PANEL, PANEL)]

    def part_copy(s, h, kind):
        p = lax.rem(s, 2)
        dst, recv, device = {
            "mid": (mid_in.at[p, h], mid_recv.at[p, h], onward),
            "acc": (acc_in.at[p, h], acc_recv.at[p, h], onward),
            "dir": (dir_in.at[p, h], dir_recv.at[p, h], {"y": plus(y, 3 - 2 * core, 4)}),
        }[kind]
        return remote(half_of(partial.at[s], h), dst, part_send.at[s, h], recv, device)

    def make_partial(s, value_of, table):
        table = packed(table)
        for source in range(4):
            value = scaled(value_of(source), source, table)
            turned[:, source * ROWS : (source + 1) * ROWS] = value.T.astype(BF16)
        hops = hops_to(s)
        for h in range(2):
            at = slice(h * PANEL, (h + 1) * PANEL)
            value = jnp.dot(turned[...], panel[:, at], preferred_element_type=F32)
            keep[s, :, at] = value
            partial[s, :, at] = value.astype(BF16)

            @pl.when(hops == 2)
            def _():
                part_copy(s, h, "mid").start()

            @pl.when(hops == 3)
            def _():
                part_copy(s, h, "dir").start()

    def add_relay(s):
        @pl.when(hops_to(s) == 1)
        def _():
            for h in range(2):
                p = lax.rem(s, 2)
                part_copy(s, h, "mid").wait_recv()
                at = slice(h * PANEL, (h + 1) * PANEL)
                partial[s, :, at] = (keep[s, :, at] + mid_in[p, h].astype(F32)).astype(BF16)
                part_copy(s, h, "acc").start()

    def from_z(d):
        s = plus(z, d, 8)
        make_partial(s, lambda source: z_raw[s, source], z_tab[s])

    make_partial(z, lambda source: raw[group, source], row_tab[group])
    z_pass(2, 3)
    z_pass(3, 1)
    from_z(7)
    from_z(1)
    add_relay(z)
    z_pass(3, 2)
    z_pass(3, 3)
    from_z(6)
    add_relay(plus(z, 7, 8))
    from_z(2)
    add_relay(plus(z, 1, 8))
    from_z(5)
    add_relay(plus(z, 6, 8))
    from_z(3)
    add_relay(plus(z, 2, 8))
    add_relay(plus(z, 5, 8))
    for slot in range(4):
        z_pass(4, slot)
    ztab_pass(4)
    from_z(4)
    add_relay(plus(z, 3, 8))
    add_relay(plus(z, 4, 8))

    def fold_copy(p, h):
        target = 2 * h + p
        d = plus(target, 4 - x, 4) - 1
        return remote(
            folded.at[p, h], out.at[pl.ds(pl.multiple_of(x * LANES, LANES), LANES)],
            fold_send.at[p, h], fold_recv.at[d], at_x(target, core),
        )

    for p in (plus(z, 1, 2), plus(z, 0, 2)):
        for h in range(2):
            s = 2 * y + p
            part_copy(s, h, "acc").wait_recv()
            part_copy(s, h, "dir").wait_recv()
            at = slice(h * PANEL, (h + 1) * PANEL)
            value = keep[s, :, at] + acc_in[p, h].astype(F32) + dir_in[p, h].astype(F32)
            value = value.astype(BF16)

            @pl.when(2 * h + p != x)
            def _():
                folded[p, h] = value
                fold_copy(p, h).start()

            @pl.when(2 * h + p == x)
            def _():
                out[pl.ds(pl.multiple_of(x * LANES, LANES), LANES), :] = value

    for d in (1, 2, 3):
        pltpu.make_async_copy(
            folded.at[0, 0], out.at[pl.ds(0, LANES)], fold_recv.at[d - 1]
        ).wait()

    for copy in drains:
        copy.wait_send()

    @pl.when(xh != core)
    def _():
        for slot in range(4):
            slice_copy(slot, 0).wait_send()
        lab_copy(0).wait_send()
        rowsum_copy(0).wait_send()

    for s in range(8):
        @pl.when(y != s // 2)
        def _():
            for h in range(2):
                part_copy(jnp.int32(s), h, "dir").wait_send()

    for p in range(2):
        for h in range(2):
            @pl.when(2 * h + p != x)
            def _():
                fold_copy(p, h).wait_send()


def shards(dosage, cohort, live_blocks, weight_counts):
    slot = lax.broadcasted_iota(jnp.int32, cohort.shape, 0) // BLOCK
    code = jnp.where(slot < live_blocks[0], cohort, -1).astype(F32).reshape(7, BLOCK)
    none = jnp.full((BLOCK,), -1.0, F32)
    labs = jnp.stack([
        jnp.concatenate([code[0], code[1], code[2], code[3]]),
        jnp.concatenate([none, code[6], code[5], code[4]]),
        jnp.concatenate([code[4], code[5], code[6], none]),
    ])
    labs = jnp.broadcast_to(labs[:, None, :], (3, COHORTS, ROWS))
    vmem = pl.BlockSpec(memory_space=pltpu.VMEM)
    smem = pl.BlockSpec(memory_space=pltpu.SMEM)

    def dma(*shape):
        return pltpu.SemaphoreType.DMA(shape)

    ld = pl.pallas_call(
        kernel,
        out_shape=jax.ShapeDtypeStruct((PANEL, PANEL), BF16),
        in_specs=[pl.BlockSpec(memory_space=pl.ANY), vmem, smem, smem],
        out_specs=vmem,
        scratch_shapes=[
            pltpu.VMEM((ROWS + SURPLUS, PANEL), BF16),
            pltpu.VMEM((3, BLOCK, PANEL), BF16),
            pltpu.VMEM((COHORTS, ROWS), F32),
            pltpu.VMEM((COHORTS, ROWS), F32),
            pltpu.VMEM((4, ROWS, LANES), BF16),
            pltpu.VMEM((8, 4, ROWS, LANES), BF16),
            pltpu.VMEM((4, COHORTS, ROWS), F32),
            pltpu.VMEM((4, ROWS, 32), BF16),
            pltpu.VMEM((4, 24, LANES), F32),
            pltpu.VMEM((4, 24, LANES), F32),
            pltpu.VMEM((24, LANES), F32),
            pltpu.VMEM((3, 24, LANES), F32),
            pltpu.VMEM((8, 16, LANES), F32),
            pltpu.VMEM((8, 16, LANES), F32),
            pltpu.VMEM((8, 4, ROWS, LANES), BF16),
            pltpu.VMEM((DEPTH, WIDTH), BF16),
            pltpu.VMEM((LANES, DEPTH), BF16),
            pltpu.VMEM((8, LANES, WIDTH), F32),
            pltpu.VMEM((8, LANES, WIDTH), BF16),
            pltpu.VMEM((2, 2, LANES, PANEL), BF16),
            pltpu.VMEM((2, 2, LANES, PANEL), BF16),
            pltpu.VMEM((2, 2, LANES, PANEL), BF16),
            pltpu.VMEM((2, 2, LANES, PANEL), BF16),
            pltpu.SemaphoreType.DMA, dma(3), dma(3),
            pltpu.SemaphoreType.DMA, pltpu.SemaphoreType.DMA,
            dma(4, 4), dma(4, 4), dma(4), dma(4), dma(4), dma(4), dma(3), dma(3),
            dma(8), dma(8), dma(2, 4), dma(2, 4),
            dma(2, 4), dma(2, 4), dma(4), dma(4), dma(4, 4), dma(4, 4),
            dma(2, 4, 4), dma(2, 4, 4), dma(8, 2), dma(2, 2), dma(2, 2), dma(2, 2),
            dma(2, 2), dma(3),
        ],
        compiler_params=pltpu.CompilerParams(
            collective_id=0, has_side_effects=True, vmem_limit_bytes=60 * 1024 * 1024
        ),
    )(dosage, labs, live_blocks, weight_counts)
    return ld.astype(F32)


def solution(mesh):
    torus = Mesh(mesh.devices.reshape(4, 2, 2, 8, 2), ("y", "xl", "co", "z", "xh"))
    samp, var = ("y", "xl", "co"), ("z", "xh")
    placed = (P(samp, var), P(samp), P(samp), P())
    return jax.shard_map(
        shards, mesh=torus, in_specs=placed, out_specs=P(samp, var), check_vma=False
    )
```

```python
import jax
import jax.numpy as jnp
from jax import lax
from jax.experimental import pallas as pl
from jax.experimental.pallas import tpu as pltpu
from jax.sharding import Mesh
from jax.sharding import PartitionSpec as P

COHORTS = 8
BLOCK = 96
HALF = 4
SURPLUS = 3 * BLOCK
ROWS = HALF * BLOCK
LANES = 128
PANEL = 512
DEPTH = 4 * ROWS
WIDTH = 2 * PANEL
EPSILON = 1e-05
MESH = pl.DeviceIdType.MESH
F32 = jnp.float32
BF16 = jnp.bfloat16


def split_three(value):
    first = value.astype(BF16)
    rest = value - first.astype(F32)
    second = rest.astype(BF16)
    third = (rest - second.astype(F32)).astype(BF16)
    return first.astype(F32), second.astype(F32), third.astype(F32)


def kernel(
    dose, labs, live, weights, out,
    own, surplus, surplus_lab, own_lab, cols,
    raw, row_labs, hot_ref, slice_sums, row_sums, sums, far_sums, row_tab, z_tab,
    z_raw, panel, turned, keep, partial, mid_in, acc_in, dir_in, folded,
    own_sem, sur_send, sur_recv, surlab_send, surlab_recv,
    slice_send, slice_recv, lab_send, lab_recv, rowsum_send, rowsum_recv, sum_send, sum_recv,
    rowtab_send, rowtab_recv, ztab_send, ztab_recv,
    ring_send, ring_recv, fwd_send, fwd_recv, core_send, core_recv,
    z_send, z_recv, part_send, mid_recv, acc_recv, dir_recv, fold_send, fold_recv,
):
    y, xl, core, z, xh = (lax.axis_index(a) for a in ("y", "xl", "co", "z", "xh"))
    x = 2 * xh + xl

    def plus(i, d, n):
        return lax.rem(i + d, n)

    def at_x(i, c):
        return {"xh": lax.div(i, 2), "xl": lax.rem(i, 2), "co": c}

    def remote(src, dst, send, recv, device):
        return pltpu.make_async_remote_copy(
            src_ref=src, dst_ref=dst, send_sem=send, recv_sem=recv,
            device_id=device, device_id_type=MESH,
        )

    take_own = pltpu.make_async_copy(dose, own, own_sem)
    take_own.start()

    barrier = pltpu.get_barrier_semaphore()
    row_peers = [(d, c) for d in range(4) for c in range(2) if d or c]
    peers = [{"y": plus(y, d, 4)} for d in (1, 2, 3)]
    peers += [{"z": plus(z, d, 8)} for d in (1, 7)]
    peers += [at_x(plus(x, d, 4), plus(core, c, 2)) for d, c in row_peers]
    for peer in peers:
        pl.semaphore_signal(barrier, inc=1, device_id=peer, device_id_type=MESH)

    take_own.wait()
    cohorts = lax.broadcasted_iota(jnp.int32, (COHORTS, ROWS), 0).astype(F32)
    totals = None
    for first, count, labels in ((0, ROWS, labs[0]), (ROWS, SURPLUS, labs[2])):
        hot = jnp.where(labels == cohorts, 1.0, 0.0).astype(F32)[:, :count]
        hots = jnp.concatenate([hot, hot], axis=0).astype(BF16)
        value = own[first : first + count, :]
        wide = value.astype(F32)
        square = wide * wide
        high = square.astype(BF16)
        low = (square - high.astype(F32)).astype(BF16)
        dots = [jnp.dot(hots, v, preferred_element_type=F32)[:COHORTS] for v in (value, high, low)]
        members = jnp.broadcast_to(jnp.sum(hot, axis=1, keepdims=True), (COHORTS, PANEL))
        part = jnp.concatenate([dots[0], dots[1] + dots[2], members], axis=0)
        totals = part if totals is None else totals + part
    for s in range(4):
        slice_sums[s] = totals[:, s * LANES : (s + 1) * LANES]
    pl.semaphore_wait(barrier, len(peers))

    drains = []

    opposite = {"y": plus(y, 2, 4)}
    onward = {"y": plus(y, 1 + 2 * core, 4)}

    def sur_copy(b):
        return remote(
            dose.at[pl.ds((6 - b) * BLOCK, BLOCK)], surplus.at[b], sur_send.at[b], sur_recv.at[b], opposite
        )

    surlab_copy = remote(labs.at[1], surplus_lab, surlab_send, surlab_recv, opposite)

    def send_surplus():
        for b in range(3):
            sur_copy(b).start()
            drains.append(sur_copy(b))
            if b == 0:
                surlab_copy.start()
                drains.append(surlab_copy)

    group = 4 * core + x
    mine = 2 * xl + core

    def band(slot):
        return pl.ds(slot * BLOCK, BLOCK)

    def slice_copy(slot, d):
        target = plus(x, d, 4)
        if slot == 0:
            src = own.at[band(0), pl.ds(pl.multiple_of(target * LANES, LANES), LANES)]
        else:
            src = cols.at[target, band(slot)]
        dst = raw.at[4 * xh + target, mine, band(slot)]
        return remote(src, dst, slice_send.at[slot, d], slice_recv.at[slot, mine], at_x(target, xh))

    def slice_local(slot):
        if slot == 0:
            src = own.at[band(0), pl.ds(pl.multiple_of(x * LANES, LANES), LANES)]
        else:
            src = cols.at[x, band(slot)]
        return pltpu.make_async_copy(src, raw.at[group, mine, band(slot)], slice_recv.at[slot, mine])

    def lab_copy(d):
        target = plus(x, d, 4)
        return remote(
            own_lab, row_labs.at[mine], lab_send.at[d], lab_recv.at[mine], at_x(target, xh)
        )

    def rowsum_copy(d):
        target = plus(x, d, 4)
        return remote(
            slice_sums.at[target], row_sums.at[mine], rowsum_send.at[d], rowsum_recv.at[mine], at_x(target, xh)
        )

    def send_row_sums():
        for d in (1, 2, 3):
            rowsum_copy(d).start()
            drains.append(rowsum_copy(d))

        @pl.when(xh != core)
        def _():
            rowsum_copy(0).start()

        @pl.when(xh == core)
        def _():
            pltpu.make_async_copy(slice_sums.at[x], row_sums.at[mine], rowsum_recv.at[mine]).start()

    def send_slices(slot):
        for d in (1, 2, 3):
            slice_copy(slot, d).start()
            drains.append(slice_copy(slot, d))

        @pl.when(xh != core)
        def _():
            slice_copy(slot, 0).start()

        @pl.when(xh == core)
        def _():
            slice_local(slot).start()

    def send_labels():
        surlab_copy.wait_recv()
        own_lab[...] = jnp.maximum(labs[0], surplus_lab[...])
        for d in (1, 2, 3):
            lab_copy(d).start()
            drains.append(lab_copy(d))

        @pl.when(xh != core)
        def _():
            lab_copy(0).start()

        @pl.when(xh == core)
        def _():
            pltpu.make_async_copy(own_lab, row_labs.at[mine], lab_recv.at[mine]).start()

    def fill_slot(slot):
        sur_copy(slot - 1).wait_recv()
        block = jnp.where(slot < live[0], own[slot * BLOCK : (slot + 1) * BLOCK, :], surplus[slot - 1])
        for s in range(4):
            cols[s, slot * BLOCK : (slot + 1) * BLOCK, :] = block[:, s * LANES : (s + 1) * LANES]
        send_slices(slot)

    def z_copy(step, way, slot):
        d = (9 - step) if way == 0 else (step - 1)
        at = plus(z, d, 8)
        dst = z_raw.at[at, :, band(slot)]
        src = raw.at[group, :, band(slot)] if step == 1 else dst
        return remote(
            src, dst, z_send.at[way, step - 1, slot], z_recv.at[way, step - 1, slot],
            {"z": plus(z, 1 if way == 0 else 7, 8)},
        )

    def goes(step, way, slot):
        return step < 4 or (slot < 2) == (way == 0)

    def z_start(step, way, slot):
        if goes(step, way, slot):
            z_copy(step, way, slot).start()
            drains.append(z_copy(step, way, slot))

    def z_pass(step, slot):
        for way in (0, 1):
            if goes(step, way, slot):
                z_copy(step, way, slot).wait_recv()
                if step < 4:
                    z_start(step + 1, way, slot)

    right, left = plus(x, 1, 4), plus(x, 3, 4)

    def ring_copy(way, slot):
        ref = raw.at[group, :, band(slot)]
        return remote(
            ref, ref, ring_send.at[way, slot], ring_recv.at[way, slot],
            at_x(right if way == 0 else left, core),
        )

    def fwd_copy(slot):
        who, to = (left, right) if slot < 2 else (right, left)
        ref = raw.at[4 * core + who, :, band(slot)]
        return remote(ref, ref, fwd_send.at[slot], fwd_recv.at[slot], at_x(to, core))

    def core_copy(d, slot):
        ref = raw.at[4 * core + plus(x, d, 4), :, band(slot)]
        return remote(ref, ref, core_send.at[d, slot], core_recv.at[d, slot], {"co": 1 - core})

    def core_start(d, slot):
        core_copy(d, slot).start()
        drains.append(core_copy(d, slot))

    def send_slot(slot):
        for source in range(4):
            pltpu.make_async_copy(
                cols.at[0, band(slot)], raw.at[group, source, band(slot)], slice_recv.at[slot, source]
            ).wait()
        for way in (0, 1):
            z_start(1, way, slot)

    def send_ring(slot):
        for way in (0, 1):
            ring_copy(way, slot).start()
            drains.append(ring_copy(way, slot))
        core_start(0, slot)

    def pass_ring(slot):
        ring_copy(0, slot).wait_recv()
        if slot < 2:
            fwd_copy(slot).start()
        core_start(3, slot)
        ring_copy(1, slot).wait_recv()
        if slot >= 2:
            fwd_copy(slot).start()
        core_start(1, slot)
        drains.append(fwd_copy(slot))

    def pass_far(slot):
        fwd_copy(slot).wait_recv()
        core_start(2, slot)

    sum_copies = [
        remote(sums, far_sums.at[d - 1], sum_send.at[d - 1], sum_recv.at[d - 1], {"y": plus(y, d, 4)})
        for d in (1, 2, 3)
    ]

    send_slices(0)
    send_row_sums()
    send_surplus()
    send_slot(0)
    for slot in (1, 2, 3):
        fill_slot(slot)
    send_labels()
    send_ring(0)
    for slot in (1, 2, 3):
        send_slot(slot)
        send_ring(slot)
    for source in range(4):
        pltpu.make_async_copy(slice_sums.at[0], row_sums.at[source], rowsum_recv.at[source]).wait()
    sums[...] = row_sums[0] + row_sums[1] + row_sums[2] + row_sums[3]
    for copy in sum_copies:
        copy.start()
        drains.append(copy)
    z_pass(1, 0)
    z_pass(1, 1)
    pass_ring(0)
    z_pass(1, 2)
    pass_ring(1)
    z_pass(1, 3)

    for copy in sum_copies:
        copy.wait_recv()
    total = sums[...] + far_sums[0] + far_sums[1] + far_sums[2]
    size = total[16:24]
    mean = total[0:8] / size
    var = total[8:16] / size - mean * mean + EPSILON
    spread = lax.rsqrt(var)
    spread = spread * (1.5 - 0.5 * var * spread * spread)
    weight = jnp.zeros((COHORTS, LANES), F32)
    all_weights = jnp.float32(0.0)
    labels = lax.broadcasted_iota(jnp.int32, (COHORTS, LANES), 0)
    for c in range(COHORTS):
        w = weights[c].astype(F32)
        all_weights = all_weights + w
        weight = jnp.where(labels == c, w, weight)
    multiplier = spread * jnp.sqrt(weight / all_weights / size)
    row_tab[group] = jnp.concatenate([mean, multiplier], axis=0)

    def rowtab_copy(d, c):
        ref = row_tab.at[group]
        return remote(
            ref, ref, rowtab_send.at[2 * d + c], rowtab_recv.at[2 * d + c],
            at_x(plus(x, d, 4), plus(core, c, 2)),
        )

    def ztab_copy(step, way):
        at = plus(z, (9 - step) if way == 0 else (step - 1), 8)
        src = row_tab.at[group] if step == 1 else z_tab.at[at]
        return remote(
            src, z_tab.at[at], ztab_send.at[way, step - 1], ztab_recv.at[way, step - 1],
            {"z": plus(z, 1 if way == 0 else 7, 8)},
        )

    def ztab_start(step, way):
        if step < 4 or way == 0:
            ztab_copy(step, way).start()
            drains.append(ztab_copy(step, way))

    def ztab_pass(step):
        for way in (0, 1):
            if step < 4 or way == 0:
                ztab_copy(step, way).wait_recv()
                if step < 4:
                    ztab_start(step + 1, way)

    for d, c in row_peers:
        rowtab_copy(d, c).start()
        drains.append(rowtab_copy(d, c))
    for way in (0, 1):
        ztab_start(1, way)

    z_pass(2, 0)
    pass_ring(2)
    z_pass(2, 1)
    pass_ring(3)
    for source in range(4):
        pltpu.make_async_copy(own_lab, row_labs.at[source], lab_recv.at[source]).wait()
    for source in range(4):
        hot = jnp.where(row_labs[source] == cohorts, 1.0, 0.0).astype(F32)
        hots = jnp.concatenate([hot, hot, hot, jnp.zeros_like(hot)], axis=0)
        hot_ref[source] = hots.T.astype(BF16)
    pass_far(0)
    z_pass(2, 2)
    pass_far(1)
    pass_far(2)
    pass_far(3)
    z_pass(2, 3)
    ztab_pass(1)

    def packed(both):
        mean, multiplier = both[:COHORTS], both[COHORTS:]
        none = jnp.zeros_like(mean)
        return jnp.concatenate([
            jnp.concatenate(list(split_three(mean)) + [none], axis=0),
            jnp.concatenate(list(split_three(multiplier)) + [none], axis=0),
        ], axis=1).astype(BF16)

    def scaled(value, source, table):
        found = jnp.dot(hot_ref[source], table, preferred_element_type=F32)
        return (value.astype(F32) - found[:, :LANES]) * found[:, LANES:]

    for d, c in row_peers:
        rowtab_copy(d, c).wait_recv()
    for d in range(4):
        for slot in range(4):
            core_copy(d, slot).wait_recv()
    z_pass(3, 0)

    def fill_panel(g, carry):
        table = packed(row_tab[g])
        at = pl.ds(pl.multiple_of(g * LANES, LANES), LANES)
        for source in range(4):
            value = scaled(raw[g, source], source, table)
            panel[source * ROWS : (source + 1) * ROWS, at] = value.astype(BF16)
        return carry

    lax.fori_loop(0, 8, fill_panel, 0)

    sign = 1 - 2 * core

    def hops_to(s):
        return lax.rem(sign * (lax.div(s, 2) - y) + 4, 4)

    def half_of(ref, h):
        return ref.at[:, pl.ds(h * PANEL, PANEL)]

    def part_copy(s, h, kind):
        p = lax.rem(s, 2)
        dst, recv, device = {
            "mid": (mid_in.at[p, h], mid_recv.at[p, h], onward),
            "acc": (acc_in.at[p, h], acc_recv.at[p, h], onward),
            "dir": (dir_in.at[p, h], dir_recv.at[p, h], {"y": plus(y, 3 - 2 * core, 4)}),
        }[kind]
        return remote(half_of(partial.at[s], h), dst, part_send.at[s, h], recv, device)

    def make_partial(s, value_of, table):
        table = packed(table)
        for source in range(4):
            value = scaled(value_of(source), source, table)
            turned[:, source * ROWS : (source + 1) * ROWS] = value.T.astype(BF16)
        hops = hops_to(s)
        for h in range(2):
            at = slice(h * PANEL, (h + 1) * PANEL)
            value = jnp.dot(turned[...], panel[:, at], preferred_element_type=F32)
            keep[s, :, at] = value
            partial[s, :, at] = value.astype(BF16)

            @pl.when(hops == 2)
            def _():
                part_copy(s, h, "mid").start()

            @pl.when(hops == 3)
            def _():
                part_copy(s, h, "dir").start()

    def add_relay(s):
        @pl.when(hops_to(s) == 1)
        def _():
            for h in range(2):
                p = lax.rem(s, 2)
                part_copy(s, h, "mid").wait_recv()
                at = slice(h * PANEL, (h + 1) * PANEL)
                partial[s, :, at] = (keep[s, :, at] + mid_in[p, h].astype(F32)).astype(BF16)
                part_copy(s, h, "acc").start()

    def from_z(d):
        s = plus(z, d, 8)
        make_partial(s, lambda source: z_raw[s, source], z_tab[s])

    z_pass(3, 1)
    z_pass(3, 2)
    make_partial(z, lambda source: raw[group, source], row_tab[group])
    z_pass(3, 3)
    ztab_pass(2)
    from_z(7)
    from_z(1)
    add_relay(z)
    ztab_pass(3)
    from_z(6)
    add_relay(plus(z, 7, 8))
    from_z(2)
    add_relay(plus(z, 1, 8))
    from_z(5)
    add_relay(plus(z, 6, 8))
    from_z(3)
    add_relay(plus(z, 2, 8))
    for slot in range(4):
        z_pass(4, slot)
    ztab_pass(4)
    from_z(4)
    add_relay(plus(z, 5, 8))
    add_relay(plus(z, 3, 8))
    add_relay(plus(z, 4, 8))

    def fold_copy(p, h):
        target = 2 * h + p
        d = plus(target, 4 - x, 4) - 1
        return remote(
            folded.at[p, h], out.at[pl.ds(pl.multiple_of(x * LANES, LANES), LANES)],
            fold_send.at[p, h], fold_recv.at[d], at_x(target, core),
        )

    for p in (plus(z, 1, 2), plus(z, 0, 2)):
        for h in range(2):
            s = 2 * y + p
            part_copy(s, h, "acc").wait_recv()
            part_copy(s, h, "dir").wait_recv()
            at = slice(h * PANEL, (h + 1) * PANEL)
            value = keep[s, :, at] + acc_in[p, h].astype(F32) + dir_in[p, h].astype(F32)
            value = value.astype(BF16)

            @pl.when(2 * h + p != x)
            def _():
                folded[p, h] = value
                fold_copy(p, h).start()

            @pl.when(2 * h + p == x)
            def _():
                out[pl.ds(pl.multiple_of(x * LANES, LANES), LANES), :] = value

    for d in (1, 2, 3):
        pltpu.make_async_copy(
            folded.at[0, 0], out.at[pl.ds(0, LANES)], fold_recv.at[d - 1]
        ).wait()

    for copy in drains:
        copy.wait_send()

    @pl.when(xh != core)
    def _():
        for slot in range(4):
            slice_copy(slot, 0).wait_send()
        lab_copy(0).wait_send()
        rowsum_copy(0).wait_send()

    for s in range(8):
        @pl.when(y != s // 2)
        def _():
            for h in range(2):
                part_copy(jnp.int32(s), h, "dir").wait_send()

    for p in range(2):
        for h in range(2):
            @pl.when(2 * h + p != x)
            def _():
                fold_copy(p, h).wait_send()


def shards(dosage, cohort, live_blocks, weight_counts):
    slot = lax.broadcasted_iota(jnp.int32, cohort.shape, 0) // BLOCK
    code = jnp.where(slot < live_blocks[0], cohort, -1).astype(F32).reshape(7, BLOCK)
    none = jnp.full((BLOCK,), -1.0, F32)
    labs = jnp.stack([
        jnp.concatenate([code[0], code[1], code[2], code[3]]),
        jnp.concatenate([none, code[6], code[5], code[4]]),
        jnp.concatenate([code[4], code[5], code[6], none]),
    ])
    labs = jnp.broadcast_to(labs[:, None, :], (3, COHORTS, ROWS))
    vmem = pl.BlockSpec(memory_space=pltpu.VMEM)
    smem = pl.BlockSpec(memory_space=pltpu.SMEM)

    def dma(*shape):
        return pltpu.SemaphoreType.DMA(shape)

    ld = pl.pallas_call(
        kernel,
        out_shape=jax.ShapeDtypeStruct((PANEL, PANEL), BF16),
        in_specs=[pl.BlockSpec(memory_space=pl.ANY), vmem, smem, smem],
        out_specs=vmem,
        scratch_shapes=[
            pltpu.VMEM((ROWS + SURPLUS, PANEL), BF16),
            pltpu.VMEM((3, BLOCK, PANEL), BF16),
            pltpu.VMEM((COHORTS, ROWS), F32),
            pltpu.VMEM((COHORTS, ROWS), F32),
            pltpu.VMEM((4, ROWS, LANES), BF16),
            pltpu.VMEM((8, 4, ROWS, LANES), BF16),
            pltpu.VMEM((4, COHORTS, ROWS), F32),
            pltpu.VMEM((4, ROWS, 32), BF16),
            pltpu.VMEM((4, 24, LANES), F32),
            pltpu.VMEM((4, 24, LANES), F32),
            pltpu.VMEM((24, LANES), F32),
            pltpu.VMEM((3, 24, LANES), F32),
            pltpu.VMEM((8, 16, LANES), F32),
            pltpu.VMEM((8, 16, LANES), F32),
            pltpu.VMEM((8, 4, ROWS, LANES), BF16),
            pltpu.VMEM((DEPTH, WIDTH), BF16),
            pltpu.VMEM((LANES, DEPTH), BF16),
            pltpu.VMEM((8, LANES, WIDTH), F32),
            pltpu.VMEM((8, LANES, WIDTH), BF16),
            pltpu.VMEM((2, 2, LANES, PANEL), BF16),
            pltpu.VMEM((2, 2, LANES, PANEL), BF16),
            pltpu.VMEM((2, 2, LANES, PANEL), BF16),
            pltpu.VMEM((2, 2, LANES, PANEL), BF16),
            pltpu.SemaphoreType.DMA, dma(3), dma(3),
            pltpu.SemaphoreType.DMA, pltpu.SemaphoreType.DMA,
            dma(4, 4), dma(4, 4), dma(4), dma(4), dma(4), dma(4), dma(3), dma(3),
            dma(8), dma(8), dma(2, 4), dma(2, 4),
            dma(2, 4), dma(2, 4), dma(4), dma(4), dma(4, 4), dma(4, 4),
            dma(2, 4, 4), dma(2, 4, 4), dma(8, 2), dma(2, 2), dma(2, 2), dma(2, 2),
            dma(2, 2), dma(3),
        ],
        compiler_params=pltpu.CompilerParams(
            collective_id=0, has_side_effects=True, vmem_limit_bytes=60 * 1024 * 1024
        ),
    )(dosage, labs, live_blocks, weight_counts)
    return ld.astype(F32)


def solution(mesh):
    torus = Mesh(mesh.devices.reshape(4, 2, 2, 8, 2), ("y", "xl", "co", "z", "xh"))
    samp, var = ("y", "xl", "co"), ("z", "xh")
    placed = (P(samp, var), P(samp), P(samp), P())
    return jax.shard_map(
        shards, mesh=torus, in_specs=placed, out_specs=P(samp, var), check_vma=False
    )
```

```python
import jax
import jax.numpy as jnp
from jax import lax
from jax.experimental import pallas as pl
from jax.experimental.pallas import tpu as pltpu
from jax.sharding import Mesh
from jax.sharding import PartitionSpec as P

COHORTS = 8
BLOCK = 96
HALF = 4
SURPLUS = 3 * BLOCK
ROWS = HALF * BLOCK
LANES = 128
PANEL = 512
DEPTH = 4 * ROWS
WIDTH = 2 * PANEL
EPSILON = 1e-05
MESH = pl.DeviceIdType.MESH
F32 = jnp.float32
BF16 = jnp.bfloat16


def split_three(value):
    first = value.astype(BF16)
    rest = value - first.astype(F32)
    second = rest.astype(BF16)
    third = (rest - second.astype(F32)).astype(BF16)
    return first.astype(F32), second.astype(F32), third.astype(F32)


def kernel(
    dose, labs, live, weights, out,
    own, surplus, surplus_lab, own_lab, cols,
    raw, row_labs, hot_ref, slice_sums, row_sums, sums, far_sums, row_tab, z_tab,
    z_raw, panel, turned, keep, partial, mid_in, acc_in, dir_in, folded,
    own_sem, sur_send, sur_recv, surlab_send, surlab_recv,
    slice_send, slice_recv, lab_send, lab_recv, rowsum_send, rowsum_recv, sum_send, sum_recv,
    rowtab_send, rowtab_recv, ztab_send, ztab_recv,
    ring_send, ring_recv, fwd_send, fwd_recv, core_send, core_recv,
    z_send, z_recv, part_send, mid_recv, acc_recv, dir_recv, fold_send, fold_recv,
):
    y, xl, core, z, xh = (lax.axis_index(a) for a in ("y", "xl", "co", "z", "xh"))
    x = 2 * xh + xl

    def plus(i, d, n):
        return lax.rem(i + d, n)

    def at_x(i, c):
        return {"xh": lax.div(i, 2), "xl": lax.rem(i, 2), "co": c}

    def remote(src, dst, send, recv, device):
        return pltpu.make_async_remote_copy(
            src_ref=src, dst_ref=dst, send_sem=send, recv_sem=recv,
            device_id=device, device_id_type=MESH,
        )

    take_own = pltpu.make_async_copy(dose, own, own_sem)
    take_own.start()

    barrier = pltpu.get_barrier_semaphore()
    row_peers = [(d, c) for d in range(4) for c in range(2) if d or c]
    peers = [{"y": plus(y, d, 4)} for d in (1, 2, 3)]
    peers += [{"z": plus(z, d, 8)} for d in (1, 7)]
    peers += [at_x(plus(x, d, 4), plus(core, c, 2)) for d, c in row_peers]
    for peer in peers:
        pl.semaphore_signal(barrier, inc=1, device_id=peer, device_id_type=MESH)

    take_own.wait()
    pl.semaphore_wait(barrier, len(peers))

    drains = []

    opposite = {"y": plus(y, 2, 4)}
    onward = {"y": plus(y, 1 + 2 * core, 4)}

    def sur_copy(b):
        return remote(
            dose.at[pl.ds((6 - b) * BLOCK, BLOCK)], surplus.at[b], sur_send.at[b], sur_recv.at[b], opposite
        )

    surlab_copy = remote(labs.at[1], surplus_lab, surlab_send, surlab_recv, opposite)

    def send_surplus():
        for b in range(3):
            sur_copy(b).start()
            drains.append(sur_copy(b))
            if b == 0:
                surlab_copy.start()
                drains.append(surlab_copy)

    group = 4 * core + x
    mine = 2 * xl + core

    def band(slot):
        return pl.ds(slot * BLOCK, BLOCK)

    def slice_copy(slot, d):
        target = plus(x, d, 4)
        if slot == 0:
            src = own.at[band(0), pl.ds(pl.multiple_of(target * LANES, LANES), LANES)]
        else:
            src = cols.at[target, band(slot)]
        dst = raw.at[4 * xh + target, mine, band(slot)]
        return remote(src, dst, slice_send.at[slot, d], slice_recv.at[slot, mine], at_x(target, xh))

    def slice_local(slot):
        if slot == 0:
            src = own.at[band(0), pl.ds(pl.multiple_of(x * LANES, LANES), LANES)]
        else:
            src = cols.at[x, band(slot)]
        return pltpu.make_async_copy(src, raw.at[group, mine, band(slot)], slice_recv.at[slot, mine])

    def lab_copy(d):
        target = plus(x, d, 4)
        return remote(
            own_lab, row_labs.at[mine], lab_send.at[d], lab_recv.at[mine], at_x(target, xh)
        )

    def rowsum_copy(d):
        target = plus(x, d, 4)
        return remote(
            slice_sums.at[target], row_sums.at[mine], rowsum_send.at[d], rowsum_recv.at[mine], at_x(target, xh)
        )

    def send_row_sums():
        for d in (1, 2, 3):
            rowsum_copy(d).start()
            drains.append(rowsum_copy(d))

        @pl.when(xh != core)
        def _():
            rowsum_copy(0).start()

        @pl.when(xh == core)
        def _():
            pltpu.make_async_copy(slice_sums.at[x], row_sums.at[mine], rowsum_recv.at[mine]).start()

    def send_slices(slot):
        for d in (1, 2, 3):
            slice_copy(slot, d).start()
            drains.append(slice_copy(slot, d))

        @pl.when(xh != core)
        def _():
            slice_copy(slot, 0).start()

        @pl.when(xh == core)
        def _():
            slice_local(slot).start()

    def send_labels():
        surlab_copy.wait_recv()
        own_lab[...] = jnp.maximum(labs[0], surplus_lab[...])
        for d in (1, 2, 3):
            lab_copy(d).start()
            drains.append(lab_copy(d))

        @pl.when(xh != core)
        def _():
            lab_copy(0).start()

        @pl.when(xh == core)
        def _():
            pltpu.make_async_copy(own_lab, row_labs.at[mine], lab_recv.at[mine]).start()

    def fill_slot(slot):
        sur_copy(slot - 1).wait_recv()
        block = jnp.where(slot < live[0], own[slot * BLOCK : (slot + 1) * BLOCK, :], surplus[slot - 1])
        for s in range(4):
            cols[s, slot * BLOCK : (slot + 1) * BLOCK, :] = block[:, s * LANES : (s + 1) * LANES]
        send_slices(slot)

    def z_copy(step, way, slot):
        d = (9 - step) if way == 0 else (step - 1)
        at = plus(z, d, 8)
        dst = z_raw.at[at, :, band(slot)]
        src = raw.at[group, :, band(slot)] if step == 1 else dst
        return remote(
            src, dst, z_send.at[way, step - 1, slot], z_recv.at[way, step - 1, slot],
            {"z": plus(z, 1 if way == 0 else 7, 8)},
        )

    def goes(step, way, slot):
        return step < 4 or (slot < 2) == (way == 0)

    def z_start(step, way, slot):
        if goes(step, way, slot):
            z_copy(step, way, slot).start()
            drains.append(z_copy(step, way, slot))

    def z_pass(step, slot):
        for way in (0, 1):
            if goes(step, way, slot):
                z_copy(step, way, slot).wait_recv()
                if step < 4:
                    z_start(step + 1, way, slot)

    right, left = plus(x, 1, 4), plus(x, 3, 4)

    def ring_copy(way, slot):
        ref = raw.at[group, :, band(slot)]
        return remote(
            ref, ref, ring_send.at[way, slot], ring_recv.at[way, slot],
            at_x(right if way == 0 else left, core),
        )

    def fwd_copy(slot):
        who, to = (left, right) if slot < 2 else (right, left)
        ref = raw.at[4 * core + who, :, band(slot)]
        return remote(ref, ref, fwd_send.at[slot], fwd_recv.at[slot], at_x(to, core))

    def core_copy(d, slot):
        ref = raw.at[4 * core + plus(x, d, 4), :, band(slot)]
        return remote(ref, ref, core_send.at[d, slot], core_recv.at[d, slot], {"co": 1 - core})

    def core_start(d, slot):
        core_copy(d, slot).start()
        drains.append(core_copy(d, slot))

    def send_slot(slot):
        for source in range(4):
            pltpu.make_async_copy(
                cols.at[0, band(slot)], raw.at[group, source, band(slot)], slice_recv.at[slot, source]
            ).wait()
        for way in (0, 1):
            z_start(1, way, slot)

    def send_ring(slot):
        for way in (0, 1):
            ring_copy(way, slot).start()
            drains.append(ring_copy(way, slot))
        core_start(0, slot)

    def pass_ring(slot):
        ring_copy(0, slot).wait_recv()
        if slot < 2:
            fwd_copy(slot).start()
        core_start(3, slot)
        ring_copy(1, slot).wait_recv()
        if slot >= 2:
            fwd_copy(slot).start()
        core_start(1, slot)
        drains.append(fwd_copy(slot))

    def pass_far(slot):
        fwd_copy(slot).wait_recv()
        core_start(2, slot)

    sum_copies = [
        remote(sums, far_sums.at[d - 1], sum_send.at[d - 1], sum_recv.at[d - 1], {"y": plus(y, d, 4)})
        for d in (1, 2, 3)
    ]

    send_slices(0)
    send_surplus()

    cohorts = lax.broadcasted_iota(jnp.int32, (COHORTS, ROWS), 0).astype(F32)
    totals = None
    for first, count, labels in ((0, ROWS, labs[0]), (ROWS, SURPLUS, labs[2])):
        hot = jnp.where(labels == cohorts, 1.0, 0.0).astype(F32)[:, :count]
        hots = jnp.concatenate([hot, hot], axis=0).astype(BF16)
        value = own[first : first + count, :]
        wide = value.astype(F32)
        square = wide * wide
        high = square.astype(BF16)
        low = (square - high.astype(F32)).astype(BF16)
        dots = [jnp.dot(hots, v, preferred_element_type=F32)[:COHORTS] for v in (value, high, low)]
        members = jnp.broadcast_to(jnp.sum(hot, axis=1, keepdims=True), (COHORTS, PANEL))
        part = jnp.concatenate([dots[0], dots[1] + dots[2], members], axis=0)
        totals = part if totals is None else totals + part
    for s in range(4):
        slice_sums[s] = totals[:, s * LANES : (s + 1) * LANES]
    send_row_sums()
    send_slot(0)
    for slot in (1, 2, 3):
        fill_slot(slot)
    send_labels()
    send_ring(0)
    for slot in (1, 2, 3):
        send_slot(slot)
        send_ring(slot)
    for source in range(4):
        pltpu.make_async_copy(slice_sums.at[0], row_sums.at[source], rowsum_recv.at[source]).wait()
    sums[...] = row_sums[0] + row_sums[1] + row_sums[2] + row_sums[3]
    for copy in sum_copies:
        copy.start()
        drains.append(copy)
    z_pass(1, 0)
    z_pass(1, 1)
    pass_ring(0)
    z_pass(1, 2)
    pass_ring(1)
    z_pass(1, 3)

    for copy in sum_copies:
        copy.wait_recv()
    total = sums[...] + far_sums[0] + far_sums[1] + far_sums[2]
    size = total[16:24]
    mean = total[0:8] / size
    var = total[8:16] / size - mean * mean + EPSILON
    spread = lax.rsqrt(var)
    spread = spread * (1.5 - 0.5 * var * spread * spread)
    weight = jnp.zeros((COHORTS, LANES), F32)
    all_weights = jnp.float32(0.0)
    labels = lax.broadcasted_iota(jnp.int32, (COHORTS, LANES), 0)
    for c in range(COHORTS):
        w = weights[c].astype(F32)
        all_weights = all_weights + w
        weight = jnp.where(labels == c, w, weight)
    multiplier = spread * jnp.sqrt(weight / all_weights / size)
    row_tab[group] = jnp.concatenate([mean, multiplier], axis=0)

    def rowtab_copy(d, c):
        ref = row_tab.at[group]
        return remote(
            ref, ref, rowtab_send.at[2 * d + c], rowtab_recv.at[2 * d + c],
            at_x(plus(x, d, 4), plus(core, c, 2)),
        )

    def ztab_copy(step, way):
        at = plus(z, (9 - step) if way == 0 else (step - 1), 8)
        src = row_tab.at[group] if step == 1 else z_tab.at[at]
        return remote(
            src, z_tab.at[at], ztab_send.at[way, step - 1], ztab_recv.at[way, step - 1],
            {"z": plus(z, 1 if way == 0 else 7, 8)},
        )

    def ztab_start(step, way):
        if step < 4 or way == 0:
            ztab_copy(step, way).start()
            drains.append(ztab_copy(step, way))

    def ztab_pass(step):
        for way in (0, 1):
            if step < 4 or way == 0:
                ztab_copy(step, way).wait_recv()
                if step < 4:
                    ztab_start(step + 1, way)

    for d, c in row_peers:
        rowtab_copy(d, c).start()
        drains.append(rowtab_copy(d, c))
    for way in (0, 1):
        ztab_start(1, way)

    z_pass(2, 0)
    pass_ring(2)
    z_pass(2, 1)
    pass_ring(3)
    for source in range(4):
        pltpu.make_async_copy(own_lab, row_labs.at[source], lab_recv.at[source]).wait()
    for source in range(4):
        hot = jnp.where(row_labs[source] == cohorts, 1.0, 0.0).astype(F32)
        hots = jnp.concatenate([hot, hot, hot, jnp.zeros_like(hot)], axis=0)
        hot_ref[source] = hots.T.astype(BF16)
    pass_far(0)
    z_pass(2, 2)
    pass_far(1)
    pass_far(2)
    pass_far(3)
    z_pass(2, 3)
    ztab_pass(1)

    def packed(both):
        mean, multiplier = both[:COHORTS], both[COHORTS:]
        none = jnp.zeros_like(mean)
        return jnp.concatenate([
            jnp.concatenate(list(split_three(mean)) + [none], axis=0),
            jnp.concatenate(list(split_three(multiplier)) + [none], axis=0),
        ], axis=1).astype(BF16)

    def scaled(value, source, table):
        found = jnp.dot(hot_ref[source], table, preferred_element_type=F32)
        return (value.astype(F32) - found[:, :LANES]) * found[:, LANES:]

    for d, c in row_peers:
        rowtab_copy(d, c).wait_recv()
    for d in range(4):
        for slot in range(4):
            core_copy(d, slot).wait_recv()
    z_pass(3, 0)

    def fill_panel(g, carry):
        table = packed(row_tab[g])
        at = pl.ds(pl.multiple_of(g * LANES, LANES), LANES)
        for source in range(4):
            value = scaled(raw[g, source], source, table)
            panel[source * ROWS : (source + 1) * ROWS, at] = value.astype(BF16)
        return carry

    lax.fori_loop(0, 8, fill_panel, 0)

    sign = 1 - 2 * core

    def hops_to(s):
        return lax.rem(sign * (lax.div(s, 2) - y) + 4, 4)

    def half_of(ref, h):
        return ref.at[:, pl.ds(h * PANEL, PANEL)]

    def part_copy(s, h, kind):
        p = lax.rem(s, 2)
        dst, recv, device = {
            "mid": (mid_in.at[p, h], mid_recv.at[p, h], onward),
            "acc": (acc_in.at[p, h], acc_recv.at[p, h], onward),
            "dir": (dir_in.at[p, h], dir_recv.at[p, h], {"y": plus(y, 3 - 2 * core, 4)}),
        }[kind]
        return remote(half_of(partial.at[s], h), dst, part_send.at[s, h], recv, device)

    def make_partial(s, value_of, table):
        table = packed(table)
        for source in range(4):
            value = scaled(value_of(source), source, table)
            turned[:, source * ROWS : (source + 1) * ROWS] = value.T.astype(BF16)
        hops = hops_to(s)
        for h in range(2):
            at = slice(h * PANEL, (h + 1) * PANEL)
            value = jnp.dot(turned[...], panel[:, at], preferred_element_type=F32)
            keep[s, :, at] = value
            partial[s, :, at] = value.astype(BF16)

            @pl.when(hops == 2)
            def _():
                part_copy(s, h, "mid").start()

            @pl.when(hops == 3)
            def _():
                part_copy(s, h, "dir").start()

    def add_relay(s):
        @pl.when(hops_to(s) == 1)
        def _():
            for h in range(2):
                p = lax.rem(s, 2)
                part_copy(s, h, "mid").wait_recv()
                at = slice(h * PANEL, (h + 1) * PANEL)
                partial[s, :, at] = (keep[s, :, at] + mid_in[p, h].astype(F32)).astype(BF16)
                part_copy(s, h, "acc").start()

    def from_z(d):
        s = plus(z, d, 8)
        make_partial(s, lambda source: z_raw[s, source], z_tab[s])

    make_partial(z, lambda source: raw[group, source], row_tab[group])
    z_pass(3, 1)
    from_z(7)
    from_z(1)
    z_pass(3, 2)
    add_relay(z)
    z_pass(3, 3)
    ztab_pass(2)
    from_z(6)
    add_relay(plus(z, 7, 8))
    from_z(2)
    add_relay(plus(z, 1, 8))
    ztab_pass(3)
    from_z(5)
    from_z(3)
    add_relay(plus(z, 6, 8))
    add_relay(plus(z, 2, 8))
    for slot in range(4):
        z_pass(4, slot)
    ztab_pass(4)
    from_z(4)
    add_relay(plus(z, 5, 8))
    add_relay(plus(z, 3, 8))
    add_relay(plus(z, 4, 8))

    def fold_copy(p, h):
        target = 2 * h + p
        d = plus(target, 4 - x, 4) - 1
        return remote(
            folded.at[p, h], out.at[pl.ds(pl.multiple_of(x * LANES, LANES), LANES)],
            fold_send.at[p, h], fold_recv.at[d], at_x(target, core),
        )

    for p in (plus(z, 1, 2), plus(z, 0, 2)):
        for h in range(2):
            s = 2 * y + p
            part_copy(s, h, "acc").wait_recv()
            part_copy(s, h, "dir").wait_recv()
            at = slice(h * PANEL, (h + 1) * PANEL)
            value = keep[s, :, at] + acc_in[p, h].astype(F32) + dir_in[p, h].astype(F32)
            value = value.astype(BF16)

            @pl.when(2 * h + p != x)
            def _():
                folded[p, h] = value
                fold_copy(p, h).start()

            @pl.when(2 * h + p == x)
            def _():
                out[pl.ds(pl.multiple_of(x * LANES, LANES), LANES), :] = value

    for d in (1, 2, 3):
        pltpu.make_async_copy(
            folded.at[0, 0], out.at[pl.ds(0, LANES)], fold_recv.at[d - 1]
        ).wait()

    for copy in drains:
        copy.wait_send()

    @pl.when(xh != core)
    def _():
        for slot in range(4):
            slice_copy(slot, 0).wait_send()
        lab_copy(0).wait_send()
        rowsum_copy(0).wait_send()

    for s in range(8):
        @pl.when(y != s // 2)
        def _():
            for h in range(2):
                part_copy(jnp.int32(s), h, "dir").wait_send()

    for p in range(2):
        for h in range(2):
            @pl.when(2 * h + p != x)
            def _():
                fold_copy(p, h).wait_send()


def shards(dosage, cohort, live_blocks, weight_counts):
    slot = lax.broadcasted_iota(jnp.int32, cohort.shape, 0) // BLOCK
    code = jnp.where(slot < live_blocks[0], cohort, -1).astype(F32).reshape(7, BLOCK)
    none = jnp.full((BLOCK,), -1.0, F32)
    labs = jnp.stack([
        jnp.concatenate([code[0], code[1], code[2], code[3]]),
        jnp.concatenate([none, code[6], code[5], code[4]]),
        jnp.concatenate([code[4], code[5], code[6], none]),
    ])
    labs = jnp.broadcast_to(labs[:, None, :], (3, COHORTS, ROWS))
    vmem = pl.BlockSpec(memory_space=pltpu.VMEM)
    smem = pl.BlockSpec(memory_space=pltpu.SMEM)

    def dma(*shape):
        return pltpu.SemaphoreType.DMA(shape)

    ld = pl.pallas_call(
        kernel,
        out_shape=jax.ShapeDtypeStruct((PANEL, PANEL), BF16),
        in_specs=[pl.BlockSpec(memory_space=pl.ANY), vmem, smem, smem],
        out_specs=vmem,
        scratch_shapes=[
            pltpu.VMEM((ROWS + SURPLUS, PANEL), BF16),
            pltpu.VMEM((3, BLOCK, PANEL), BF16),
            pltpu.VMEM((COHORTS, ROWS), F32),
            pltpu.VMEM((COHORTS, ROWS), F32),
            pltpu.VMEM((4, ROWS, LANES), BF16),
            pltpu.VMEM((8, 4, ROWS, LANES), BF16),
            pltpu.VMEM((4, COHORTS, ROWS), F32),
            pltpu.VMEM((4, ROWS, 32), BF16),
            pltpu.VMEM((4, 24, LANES), F32),
            pltpu.VMEM((4, 24, LANES), F32),
            pltpu.VMEM((24, LANES), F32),
            pltpu.VMEM((3, 24, LANES), F32),
            pltpu.VMEM((8, 16, LANES), F32),
            pltpu.VMEM((8, 16, LANES), F32),
            pltpu.VMEM((8, 4, ROWS, LANES), BF16),
            pltpu.VMEM((DEPTH, WIDTH), BF16),
            pltpu.VMEM((LANES, DEPTH), BF16),
            pltpu.VMEM((8, LANES, WIDTH), F32),
            pltpu.VMEM((8, LANES, WIDTH), BF16),
            pltpu.VMEM((2, 2, LANES, PANEL), BF16),
            pltpu.VMEM((2, 2, LANES, PANEL), BF16),
            pltpu.VMEM((2, 2, LANES, PANEL), BF16),
            pltpu.VMEM((2, 2, LANES, PANEL), BF16),
            pltpu.SemaphoreType.DMA, dma(3), dma(3),
            pltpu.SemaphoreType.DMA, pltpu.SemaphoreType.DMA,
            dma(4, 4), dma(4, 4), dma(4), dma(4), dma(4), dma(4), dma(3), dma(3),
            dma(8), dma(8), dma(2, 4), dma(2, 4),
            dma(2, 4), dma(2, 4), dma(4), dma(4), dma(4, 4), dma(4, 4),
            dma(2, 4, 4), dma(2, 4, 4), dma(8, 2), dma(2, 2), dma(2, 2), dma(2, 2),
            dma(2, 2), dma(3),
        ],
        compiler_params=pltpu.CompilerParams(
            collective_id=0, has_side_effects=True, vmem_limit_bytes=60 * 1024 * 1024
        ),
    )(dosage, labs, live_blocks, weight_counts)
    return ld.astype(F32)


def solution(mesh):
    torus = Mesh(mesh.devices.reshape(4, 2, 2, 8, 2), ("y", "xl", "co", "z", "xh"))
    samp, var = ("y", "xl", "co"), ("z", "xh")
    placed = (P(samp, var), P(samp), P(samp), P())
    return jax.shard_map(
        shards, mesh=torus, in_specs=placed, out_specs=P(samp, var), check_vma=False
    )
```

```python
import jax
import jax.numpy as jnp
from jax import lax
from jax.experimental import pallas as pl
from jax.experimental.pallas import tpu as pltpu
from jax.sharding import Mesh
from jax.sharding import PartitionSpec as P

COHORTS = 8
BLOCK = 96
HALF = 4
SURPLUS = 3 * BLOCK
ROWS = HALF * BLOCK
LANES = 128
PANEL = 512
DEPTH = 4 * ROWS
WIDTH = 2 * PANEL
EPSILON = 1e-05
MESH = pl.DeviceIdType.MESH
F32 = jnp.float32
BF16 = jnp.bfloat16


def split_three(value):
    first = value.astype(BF16)
    rest = value - first.astype(F32)
    second = rest.astype(BF16)
    third = (rest - second.astype(F32)).astype(BF16)
    return first.astype(F32), second.astype(F32), third.astype(F32)


def kernel(
    dose, labs, live, weights, out,
    own, surplus, surplus_lab, own_lab, cols,
    raw, row_labs, hot_ref, slice_sums, row_sums, sums, far_sums, row_tab, z_tab,
    z_raw, panel, turned, keep, partial, mid_in, acc_in, dir_in, folded,
    own_sem, sur_send, sur_recv, surlab_send, surlab_recv,
    slice_send, slice_recv, lab_send, lab_recv, rowsum_send, rowsum_recv, sum_send, sum_recv,
    rowtab_send, rowtab_recv, ztab_send, ztab_recv,
    ring_send, ring_recv, fwd_send, fwd_recv, core_send, core_recv,
    z_send, z_recv, part_send, mid_recv, acc_recv, dir_recv, fold_send, fold_recv,
):
    y, xl, core, z, xh = (lax.axis_index(a) for a in ("y", "xl", "co", "z", "xh"))
    x = 2 * xh + xl

    def plus(i, d, n):
        return lax.rem(i + d, n)

    def at_x(i, c):
        return {"xh": lax.div(i, 2), "xl": lax.rem(i, 2), "co": c}

    def remote(src, dst, send, recv, device):
        return pltpu.make_async_remote_copy(
            src_ref=src, dst_ref=dst, send_sem=send, recv_sem=recv,
            device_id=device, device_id_type=MESH,
        )

    take_own = pltpu.make_async_copy(dose, own, own_sem)
    take_own.start()

    barrier = pltpu.get_barrier_semaphore()
    row_peers = [(d, c) for d in range(4) for c in range(2) if d or c]
    peers = [{"y": plus(y, d, 4)} for d in (1, 2, 3)]
    peers += [{"z": plus(z, d, 8)} for d in (1, 7)]
    peers += [at_x(plus(x, d, 4), plus(core, c, 2)) for d, c in row_peers]
    for peer in peers:
        pl.semaphore_signal(barrier, inc=1, device_id=peer, device_id_type=MESH)

    take_own.wait()
    pl.semaphore_wait(barrier, len(peers))

    drains = []

    opposite = {"y": plus(y, 2, 4)}
    onward = {"y": plus(y, 1 + 2 * core, 4)}

    def sur_copy(b):
        return remote(
            dose.at[pl.ds((6 - b) * BLOCK, BLOCK)], surplus.at[b], sur_send.at[b], sur_recv.at[b], opposite
        )

    surlab_copy = remote(labs.at[1], surplus_lab, surlab_send, surlab_recv, opposite)

    def send_surplus():
        for b in range(3):
            sur_copy(b).start()
            drains.append(sur_copy(b))
            if b == 0:
                surlab_copy.start()
                drains.append(surlab_copy)

    group = 4 * core + x
    mine = 2 * xl + core

    def band(slot):
        return pl.ds(slot * BLOCK, BLOCK)

    def slice_copy(slot, d):
        target = plus(x, d, 4)
        if slot == 0:
            src = own.at[band(0), pl.ds(pl.multiple_of(target * LANES, LANES), LANES)]
        else:
            src = cols.at[target, band(slot)]
        dst = raw.at[4 * xh + target, mine, band(slot)]
        return remote(src, dst, slice_send.at[slot, d], slice_recv.at[slot, mine], at_x(target, xh))

    def slice_local(slot):
        if slot == 0:
            src = own.at[band(0), pl.ds(pl.multiple_of(x * LANES, LANES), LANES)]
        else:
            src = cols.at[x, band(slot)]
        return pltpu.make_async_copy(src, raw.at[group, mine, band(slot)], slice_recv.at[slot, mine])

    def lab_copy(d):
        target = plus(x, d, 4)
        return remote(
            own_lab, row_labs.at[mine], lab_send.at[d], lab_recv.at[mine], at_x(target, xh)
        )

    def rowsum_copy(d):
        target = plus(x, d, 4)
        return remote(
            slice_sums.at[target], row_sums.at[mine], rowsum_send.at[d], rowsum_recv.at[mine], at_x(target, xh)
        )

    def send_row_sums():
        for d in (1, 2, 3):
            rowsum_copy(d).start()
            drains.append(rowsum_copy(d))

        @pl.when(xh != core)
        def _():
            rowsum_copy(0).start()

        @pl.when(xh == core)
        def _():
            pltpu.make_async_copy(slice_sums.at[x], row_sums.at[mine], rowsum_recv.at[mine]).start()

    def send_slices(slot):
        for d in (1, 2, 3):
            slice_copy(slot, d).start()
            drains.append(slice_copy(slot, d))

        @pl.when(xh != core)
        def _():
            slice_copy(slot, 0).start()

        @pl.when(xh == core)
        def _():
            slice_local(slot).start()

    def send_labels():
        surlab_copy.wait_recv()
        own_lab[...] = jnp.maximum(labs[0], surplus_lab[...])
        for d in (1, 2, 3):
            lab_copy(d).start()
            drains.append(lab_copy(d))

        @pl.when(xh != core)
        def _():
            lab_copy(0).start()

        @pl.when(xh == core)
        def _():
            pltpu.make_async_copy(own_lab, row_labs.at[mine], lab_recv.at[mine]).start()

    def fill_slot(slot):
        sur_copy(slot - 1).wait_recv()
        block = jnp.where(slot < live[0], own[slot * BLOCK : (slot + 1) * BLOCK, :], surplus[slot - 1])
        for s in range(4):
            cols[s, slot * BLOCK : (slot + 1) * BLOCK, :] = block[:, s * LANES : (s + 1) * LANES]
        send_slices(slot)

    def z_copy(step, way, slot):
        d = (9 - step) if way == 0 else (step - 1)
        at = plus(z, d, 8)
        dst = z_raw.at[at, :, band(slot)]
        src = raw.at[group, :, band(slot)] if step == 1 else dst
        return remote(
            src, dst, z_send.at[way, step - 1, slot], z_recv.at[way, step - 1, slot],
            {"z": plus(z, 1 if way == 0 else 7, 8)},
        )

    def goes(step, way, slot):
        return step < 4 or (slot < 2) == (way == 0)

    def z_start(step, way, slot):
        if goes(step, way, slot):
            z_copy(step, way, slot).start()
            drains.append(z_copy(step, way, slot))

    def z_pass(step, slot):
        for way in (0, 1):
            if goes(step, way, slot):
                z_copy(step, way, slot).wait_recv()
                if step < 4:
                    z_start(step + 1, way, slot)

    right, left = plus(x, 1, 4), plus(x, 3, 4)

    def ring_copy(way, slot):
        ref = raw.at[group, :, band(slot)]
        return remote(
            ref, ref, ring_send.at[way, slot], ring_recv.at[way, slot],
            at_x(right if way == 0 else left, core),
        )

    def fwd_copy(slot):
        who, to = (left, right) if slot < 2 else (right, left)
        ref = raw.at[4 * core + who, :, band(slot)]
        return remote(ref, ref, fwd_send.at[slot], fwd_recv.at[slot], at_x(to, core))

    def core_copy(d, slot):
        ref = raw.at[4 * core + plus(x, d, 4), :, band(slot)]
        return remote(ref, ref, core_send.at[d, slot], core_recv.at[d, slot], {"co": 1 - core})

    def core_start(d, slot):
        core_copy(d, slot).start()
        drains.append(core_copy(d, slot))

    def send_slot(slot):
        for source in range(4):
            pltpu.make_async_copy(
                cols.at[0, band(slot)], raw.at[group, source, band(slot)], slice_recv.at[slot, source]
            ).wait()
        for way in (0, 1):
            z_start(1, way, slot)

    def send_ring(slot):
        for way in (0, 1):
            ring_copy(way, slot).start()
            drains.append(ring_copy(way, slot))
        core_start(0, slot)

    def pass_ring(slot):
        ring_copy(0, slot).wait_recv()
        if slot < 2:
            fwd_copy(slot).start()
        core_start(3, slot)
        ring_copy(1, slot).wait_recv()
        if slot >= 2:
            fwd_copy(slot).start()
        core_start(1, slot)
        drains.append(fwd_copy(slot))

    def pass_far(slot):
        fwd_copy(slot).wait_recv()
        core_start(2, slot)

    sum_copies = [
        remote(sums, far_sums.at[d - 1], sum_send.at[d - 1], sum_recv.at[d - 1], {"y": plus(y, d, 4)})
        for d in (1, 2, 3)
    ]

    send_slices(0)
    send_surplus()

    cohorts = lax.broadcasted_iota(jnp.int32, (COHORTS, ROWS), 0).astype(F32)
    totals = None
    for first, count, labels in ((0, ROWS, labs[0]), (ROWS, SURPLUS, labs[2])):
        hot = jnp.where(labels == cohorts, 1.0, 0.0).astype(F32)[:, :count]
        hots = jnp.concatenate([hot, hot], axis=0).astype(BF16)
        value = own[first : first + count, :]
        wide = value.astype(F32)
        square = wide * wide
        high = square.astype(BF16)
        low = (square - high.astype(F32)).astype(BF16)
        dots = [jnp.dot(hots, v, preferred_element_type=F32)[:COHORTS] for v in (value, high, low)]
        members = jnp.broadcast_to(jnp.sum(hot, axis=1, keepdims=True), (COHORTS, PANEL))
        part = jnp.concatenate([dots[0], dots[1] + dots[2], members], axis=0)
        totals = part if totals is None else totals + part
    for s in range(4):
        slice_sums[s] = totals[:, s * LANES : (s + 1) * LANES]
    send_row_sums()
    send_slot(0)
    for slot in (1, 2, 3):
        fill_slot(slot)
    send_labels()
    send_ring(0)
    for slot in (1, 2, 3):
        send_slot(slot)
        send_ring(slot)
    for source in range(4):
        pltpu.make_async_copy(slice_sums.at[0], row_sums.at[source], rowsum_recv.at[source]).wait()
    sums[...] = row_sums[0] + row_sums[1] + row_sums[2] + row_sums[3]
    for copy in sum_copies:
        copy.start()
        drains.append(copy)
    z_pass(1, 0)
    z_pass(1, 1)
    pass_ring(0)
    z_pass(1, 2)
    pass_ring(1)
    z_pass(1, 3)

    for copy in sum_copies:
        copy.wait_recv()
    total = sums[...] + far_sums[0] + far_sums[1] + far_sums[2]
    size = total[16:24]
    mean = total[0:8] / size
    var = total[8:16] / size - mean * mean + EPSILON
    spread = lax.rsqrt(var)
    spread = spread * (1.5 - 0.5 * var * spread * spread)
    weight = jnp.zeros((COHORTS, LANES), F32)
    all_weights = jnp.float32(0.0)
    labels = lax.broadcasted_iota(jnp.int32, (COHORTS, LANES), 0)
    for c in range(COHORTS):
        w = weights[c].astype(F32)
        all_weights = all_weights + w
        weight = jnp.where(labels == c, w, weight)
    multiplier = spread * jnp.sqrt(weight / all_weights / size)
    row_tab[group] = jnp.concatenate([mean, multiplier], axis=0)

    def rowtab_copy(d, c):
        ref = row_tab.at[group]
        return remote(
            ref, ref, rowtab_send.at[2 * d + c], rowtab_recv.at[2 * d + c],
            at_x(plus(x, d, 4), plus(core, c, 2)),
        )

    def ztab_copy(step, way):
        at = plus(z, (9 - step) if way == 0 else (step - 1), 8)
        src = row_tab.at[group] if step == 1 else z_tab.at[at]
        return remote(
            src, z_tab.at[at], ztab_send.at[way, step - 1], ztab_recv.at[way, step - 1],
            {"z": plus(z, 1 if way == 0 else 7, 8)},
        )

    def ztab_start(step, way):
        if step < 4 or way == 0:
            ztab_copy(step, way).start()
            drains.append(ztab_copy(step, way))

    def ztab_pass(step):
        for way in (0, 1):
            if step < 4 or way == 0:
                ztab_copy(step, way).wait_recv()
                if step < 4:
                    ztab_start(step + 1, way)

    for d, c in row_peers:
        rowtab_copy(d, c).start()
        drains.append(rowtab_copy(d, c))
    for way in (0, 1):
        ztab_start(1, way)

    z_pass(2, 0)
    pass_ring(2)
    z_pass(2, 1)
    pass_ring(3)
    for source in range(4):
        pltpu.make_async_copy(own_lab, row_labs.at[source], lab_recv.at[source]).wait()
    for source in range(4):
        hot = jnp.where(row_labs[source] == cohorts, 1.0, 0.0).astype(F32)
        hots = jnp.concatenate([hot, hot, hot, jnp.zeros_like(hot)], axis=0)
        hot_ref[source] = hots.T.astype(BF16)
    pass_far(0)
    z_pass(2, 2)
    pass_far(1)
    pass_far(2)
    pass_far(3)
    z_pass(2, 3)
    ztab_pass(1)

    def packed(both):
        mean, multiplier = both[:COHORTS], both[COHORTS:]
        none = jnp.zeros_like(mean)
        return jnp.concatenate([
            jnp.concatenate(list(split_three(mean)) + [none], axis=0),
            jnp.concatenate(list(split_three(multiplier)) + [none], axis=0),
        ], axis=1).astype(BF16)

    def scaled(value, source, table):
        found = jnp.dot(hot_ref[source], table, preferred_element_type=F32)
        return (value.astype(F32) - found[:, :LANES]) * found[:, LANES:]

    for d, c in row_peers:
        rowtab_copy(d, c).wait_recv()
    for d in range(4):
        for slot in range(4):
            core_copy(d, slot).wait_recv()
    z_pass(3, 0)

    def fill_panel(g, carry):
        table = packed(row_tab[g])
        at = pl.ds(pl.multiple_of(g * LANES, LANES), LANES)
        for source in range(4):
            value = scaled(raw[g, source], source, table)
            panel[source * ROWS : (source + 1) * ROWS, at] = value.astype(BF16)
        return carry

    lax.fori_loop(0, 8, fill_panel, 0)

    sign = 1 - 2 * core

    def hops_to(s):
        return lax.rem(sign * (lax.div(s, 2) - y) + 4, 4)

    def half_of(ref, h):
        return ref.at[:, pl.ds(h * PANEL, PANEL)]

    def part_copy(s, h, kind):
        p = lax.rem(s, 2)
        dst, recv, device = {
            "mid": (mid_in.at[p, h], mid_recv.at[p, h], onward),
            "acc": (acc_in.at[p, h], acc_recv.at[p, h], onward),
            "dir": (dir_in.at[p, h], dir_recv.at[p, h], {"y": plus(y, 3 - 2 * core, 4)}),
        }[kind]
        return remote(half_of(partial.at[s], h), dst, part_send.at[s, h], recv, device)

    def make_partial(s, value_of, table):
        table = packed(table)
        for source in range(4):
            value = scaled(value_of(source), source, table)
            turned[:, source * ROWS : (source + 1) * ROWS] = value.T.astype(BF16)
        hops = hops_to(s)
        for h in range(2):
            at = slice(h * PANEL, (h + 1) * PANEL)
            value = jnp.dot(turned[...], panel[:, at], preferred_element_type=F32)
            keep[s, :, at] = value
            partial[s, :, at] = value.astype(BF16)

            @pl.when(hops == 2)
            def _():
                part_copy(s, h, "mid").start()

            @pl.when(hops == 3)
            def _():
                part_copy(s, h, "dir").start()

    def add_relay(s):
        @pl.when(hops_to(s) == 1)
        def _():
            for h in range(2):
                p = lax.rem(s, 2)
                part_copy(s, h, "mid").wait_recv()
                at = slice(h * PANEL, (h + 1) * PANEL)
                partial[s, :, at] = (keep[s, :, at] + mid_in[p, h].astype(F32)).astype(BF16)
                part_copy(s, h, "acc").start()

    def from_z(d):
        s = plus(z, d, 8)
        make_partial(s, lambda source: z_raw[s, source], z_tab[s])

    make_partial(z, lambda source: raw[group, source], row_tab[group])
    z_pass(3, 1)
    from_z(7)
    from_z(1)
    z_pass(3, 2)
    ztab_pass(2)
    z_pass(3, 3)
    from_z(6)
    from_z(2)
    add_relay(z)
    ztab_pass(3)
    from_z(5)
    add_relay(plus(z, 7, 8))
    from_z(3)
    add_relay(plus(z, 1, 8))
    for slot in range(4):
        z_pass(4, slot)
    ztab_pass(4)
    from_z(4)
    add_relay(plus(z, 6, 8))
    add_relay(plus(z, 2, 8))
    add_relay(plus(z, 5, 8))
    add_relay(plus(z, 3, 8))
    add_relay(plus(z, 4, 8))

    def fold_copy(p, h):
        target = 2 * h + p
        d = plus(target, 4 - x, 4) - 1
        return remote(
            folded.at[p, h], out.at[pl.ds(pl.multiple_of(x * LANES, LANES), LANES)],
            fold_send.at[p, h], fold_recv.at[d], at_x(target, core),
        )

    for p in (plus(z, 1, 2), plus(z, 0, 2)):
        for h in range(2):
            s = 2 * y + p
            part_copy(s, h, "acc").wait_recv()
            part_copy(s, h, "dir").wait_recv()
            at = slice(h * PANEL, (h + 1) * PANEL)
            value = keep[s, :, at] + acc_in[p, h].astype(F32) + dir_in[p, h].astype(F32)
            value = value.astype(BF16)

            @pl.when(2 * h + p != x)
            def _():
                folded[p, h] = value
                fold_copy(p, h).start()

            @pl.when(2 * h + p == x)
            def _():
                out[pl.ds(pl.multiple_of(x * LANES, LANES), LANES), :] = value

    for d in (1, 2, 3):
        pltpu.make_async_copy(
            folded.at[0, 0], out.at[pl.ds(0, LANES)], fold_recv.at[d - 1]
        ).wait()

    for copy in drains:
        copy.wait_send()

    @pl.when(xh != core)
    def _():
        for slot in range(4):
            slice_copy(slot, 0).wait_send()
        lab_copy(0).wait_send()
        rowsum_copy(0).wait_send()

    for s in range(8):
        @pl.when(y != s // 2)
        def _():
            for h in range(2):
                part_copy(jnp.int32(s), h, "dir").wait_send()

    for p in range(2):
        for h in range(2):
            @pl.when(2 * h + p != x)
            def _():
                fold_copy(p, h).wait_send()


def shards(dosage, cohort, live_blocks, weight_counts):
    slot = lax.broadcasted_iota(jnp.int32, cohort.shape, 0) // BLOCK
    code = jnp.where(slot < live_blocks[0], cohort, -1).astype(F32).reshape(7, BLOCK)
    none = jnp.full((BLOCK,), -1.0, F32)
    labs = jnp.stack([
        jnp.concatenate([code[0], code[1], code[2], code[3]]),
        jnp.concatenate([none, code[6], code[5], code[4]]),
        jnp.concatenate([code[4], code[5], code[6], none]),
    ])
    labs = jnp.broadcast_to(labs[:, None, :], (3, COHORTS, ROWS))
    vmem = pl.BlockSpec(memory_space=pltpu.VMEM)
    smem = pl.BlockSpec(memory_space=pltpu.SMEM)

    def dma(*shape):
        return pltpu.SemaphoreType.DMA(shape)

    ld = pl.pallas_call(
        kernel,
        out_shape=jax.ShapeDtypeStruct((PANEL, PANEL), BF16),
        in_specs=[pl.BlockSpec(memory_space=pl.ANY), vmem, smem, smem],
        out_specs=vmem,
        scratch_shapes=[
            pltpu.VMEM((ROWS + SURPLUS, PANEL), BF16),
            pltpu.VMEM((3, BLOCK, PANEL), BF16),
            pltpu.VMEM((COHORTS, ROWS), F32),
            pltpu.VMEM((COHORTS, ROWS), F32),
            pltpu.VMEM((4, ROWS, LANES), BF16),
            pltpu.VMEM((8, 4, ROWS, LANES), BF16),
            pltpu.VMEM((4, COHORTS, ROWS), F32),
            pltpu.VMEM((4, ROWS, 32), BF16),
            pltpu.VMEM((4, 24, LANES), F32),
            pltpu.VMEM((4, 24, LANES), F32),
            pltpu.VMEM((24, LANES), F32),
            pltpu.VMEM((3, 24, LANES), F32),
            pltpu.VMEM((8, 16, LANES), F32),
            pltpu.VMEM((8, 16, LANES), F32),
            pltpu.VMEM((8, 4, ROWS, LANES), BF16),
            pltpu.VMEM((DEPTH, WIDTH), BF16),
            pltpu.VMEM((LANES, DEPTH), BF16),
            pltpu.VMEM((8, LANES, WIDTH), F32),
            pltpu.VMEM((8, LANES, WIDTH), BF16),
            pltpu.VMEM((2, 2, LANES, PANEL), BF16),
            pltpu.VMEM((2, 2, LANES, PANEL), BF16),
            pltpu.VMEM((2, 2, LANES, PANEL), BF16),
            pltpu.VMEM((2, 2, LANES, PANEL), BF16),
            pltpu.SemaphoreType.DMA, dma(3), dma(3),
            pltpu.SemaphoreType.DMA, pltpu.SemaphoreType.DMA,
            dma(4, 4), dma(4, 4), dma(4), dma(4), dma(4), dma(4), dma(3), dma(3),
            dma(8), dma(8), dma(2, 4), dma(2, 4),
            dma(2, 4), dma(2, 4), dma(4), dma(4), dma(4, 4), dma(4, 4),
            dma(2, 4, 4), dma(2, 4, 4), dma(8, 2), dma(2, 2), dma(2, 2), dma(2, 2),
            dma(2, 2), dma(3),
        ],
        compiler_params=pltpu.CompilerParams(
            collective_id=0, has_side_effects=True, vmem_limit_bytes=60 * 1024 * 1024
        ),
    )(dosage, labs, live_blocks, weight_counts)
    return ld.astype(F32)


def solution(mesh):
    torus = Mesh(mesh.devices.reshape(4, 2, 2, 8, 2), ("y", "xl", "co", "z", "xh"))
    samp, var = ("y", "xl", "co"), ("z", "xh")
    placed = (P(samp, var), P(samp), P(samp), P())
    return jax.shard_map(
        shards, mesh=torus, in_specs=placed, out_specs=P(samp, var), check_vma=False
    )
```

```python
import jax
import jax.numpy as jnp
from jax import lax
from jax.experimental import pallas as pl
from jax.experimental.pallas import tpu as pltpu
from jax.sharding import Mesh
from jax.sharding import PartitionSpec as P

COHORTS = 8
BLOCK = 96
HALF = 4
SURPLUS = 3 * BLOCK
ROWS = HALF * BLOCK
LANES = 128
PANEL = 512
DEPTH = 4 * ROWS
WIDTH = 2 * PANEL
EPSILON = 1e-05
MESH = pl.DeviceIdType.MESH
F32 = jnp.float32
BF16 = jnp.bfloat16


def split_three(value):
    first = value.astype(BF16)
    rest = value - first.astype(F32)
    second = rest.astype(BF16)
    third = (rest - second.astype(F32)).astype(BF16)
    return first.astype(F32), second.astype(F32), third.astype(F32)


def kernel(
    dose, labs, live, weights, out,
    own, surplus, surplus_lab, own_lab, cols,
    raw, row_labs, hot_ref, slice_sums, row_sums, sums, far_sums, row_tab, z_tab,
    z_raw, panel, turned, keep, partial, mid_in, acc_in, dir_in, folded,
    own_sem, sur_send, sur_recv, surlab_send, surlab_recv,
    slice_send, slice_recv, lab_send, lab_recv, rowsum_send, rowsum_recv, sum_send, sum_recv,
    rowtab_send, rowtab_recv, ztab_send, ztab_recv,
    ring_send, ring_recv, fwd_send, fwd_recv, core_send, core_recv,
    z_send, z_recv, part_send, mid_recv, acc_recv, dir_recv, fold_send, fold_recv,
):
    y, xl, core, z, xh = (lax.axis_index(a) for a in ("y", "xl", "co", "z", "xh"))
    x = 2 * xh + xl

    def plus(i, d, n):
        return lax.rem(i + d, n)

    def at_x(i, c):
        return {"xh": lax.div(i, 2), "xl": lax.rem(i, 2), "co": c}

    def remote(src, dst, send, recv, device):
        return pltpu.make_async_remote_copy(
            src_ref=src, dst_ref=dst, send_sem=send, recv_sem=recv,
            device_id=device, device_id_type=MESH,
        )

    take_own = pltpu.make_async_copy(dose, own, own_sem)
    take_own.start()

    barrier = pltpu.get_barrier_semaphore()
    row_peers = [(d, c) for d in range(4) for c in range(2) if d or c]
    peers = [{"y": plus(y, d, 4)} for d in (1, 2, 3)]
    peers += [{"z": plus(z, d, 8)} for d in (1, 7)]
    peers += [at_x(plus(x, d, 4), plus(core, c, 2)) for d, c in row_peers]
    for peer in peers:
        pl.semaphore_signal(barrier, inc=1, device_id=peer, device_id_type=MESH)

    take_own.wait()
    pl.semaphore_wait(barrier, len(peers))

    drains = []

    opposite = {"y": plus(y, 2, 4)}
    onward = {"y": plus(y, 1 + 2 * core, 4)}

    def sur_copy(b):
        return remote(
            dose.at[pl.ds((6 - b) * BLOCK, BLOCK)], surplus.at[b], sur_send.at[b], sur_recv.at[b], opposite
        )

    surlab_copy = remote(labs.at[1], surplus_lab, surlab_send, surlab_recv, opposite)

    def send_surplus():
        for b in range(3):
            sur_copy(b).start()
            drains.append(sur_copy(b))
            if b == 0:
                surlab_copy.start()
                drains.append(surlab_copy)

    group = 4 * core + x
    mine = 2 * xl + core

    def band(slot):
        return pl.ds(slot * BLOCK, BLOCK)

    def slice_copy(slot, d):
        target = plus(x, d, 4)
        if slot == 0:
            src = own.at[band(0), pl.ds(pl.multiple_of(target * LANES, LANES), LANES)]
        else:
            src = cols.at[target, band(slot)]
        dst = raw.at[4 * xh + target, mine, band(slot)]
        return remote(src, dst, slice_send.at[slot, d], slice_recv.at[slot, mine], at_x(target, xh))

    def slice_local(slot):
        if slot == 0:
            src = own.at[band(0), pl.ds(pl.multiple_of(x * LANES, LANES), LANES)]
        else:
            src = cols.at[x, band(slot)]
        return pltpu.make_async_copy(src, raw.at[group, mine, band(slot)], slice_recv.at[slot, mine])

    def lab_copy(d):
        target = plus(x, d, 4)
        return remote(
            own_lab, row_labs.at[mine], lab_send.at[d], lab_recv.at[mine], at_x(target, xh)
        )

    def rowsum_copy(d):
        target = plus(x, d, 4)
        return remote(
            slice_sums.at[target], row_sums.at[mine], rowsum_send.at[d], rowsum_recv.at[mine], at_x(target, xh)
        )

    def send_row_sums():
        for d in (1, 2, 3):
            rowsum_copy(d).start()
            drains.append(rowsum_copy(d))

        @pl.when(xh != core)
        def _():
            rowsum_copy(0).start()

        @pl.when(xh == core)
        def _():
            pltpu.make_async_copy(slice_sums.at[x], row_sums.at[mine], rowsum_recv.at[mine]).start()

    def send_slices(slot):
        for d in (1, 2, 3):
            slice_copy(slot, d).start()
            drains.append(slice_copy(slot, d))

        @pl.when(xh != core)
        def _():
            slice_copy(slot, 0).start()

        @pl.when(xh == core)
        def _():
            slice_local(slot).start()

    def send_labels():
        surlab_copy.wait_recv()
        own_lab[...] = jnp.maximum(labs[0], surplus_lab[...])
        for d in (1, 2, 3):
            lab_copy(d).start()
            drains.append(lab_copy(d))

        @pl.when(xh != core)
        def _():
            lab_copy(0).start()

        @pl.when(xh == core)
        def _():
            pltpu.make_async_copy(own_lab, row_labs.at[mine], lab_recv.at[mine]).start()

    def fill_slot(slot):
        sur_copy(slot - 1).wait_recv()
        block = jnp.where(slot < live[0], own[slot * BLOCK : (slot + 1) * BLOCK, :], surplus[slot - 1])
        for s in range(4):
            cols[s, slot * BLOCK : (slot + 1) * BLOCK, :] = block[:, s * LANES : (s + 1) * LANES]
        send_slices(slot)

    def z_copy(step, way, slot):
        d = (9 - step) if way == 0 else (step - 1)
        at = plus(z, d, 8)
        dst = z_raw.at[at, :, band(slot)]
        src = raw.at[group, :, band(slot)] if step == 1 else dst
        return remote(
            src, dst, z_send.at[way, step - 1, slot], z_recv.at[way, step - 1, slot],
            {"z": plus(z, 1 if way == 0 else 7, 8)},
        )

    def goes(step, way, slot):
        return step < 4 or (slot < 2) == (way == 0)

    def z_start(step, way, slot):
        if goes(step, way, slot):
            z_copy(step, way, slot).start()
            drains.append(z_copy(step, way, slot))

    def z_pass(step, slot):
        for way in (0, 1):
            if goes(step, way, slot):
                z_copy(step, way, slot).wait_recv()
                if step < 4:
                    z_start(step + 1, way, slot)

    right, left = plus(x, 1, 4), plus(x, 3, 4)

    def ring_copy(way, slot):
        ref = raw.at[group, :, band(slot)]
        return remote(
            ref, ref, ring_send.at[way, slot], ring_recv.at[way, slot],
            at_x(right if way == 0 else left, core),
        )

    def fwd_copy(slot):
        who, to = (left, right) if slot < 2 else (right, left)
        ref = raw.at[4 * core + who, :, band(slot)]
        return remote(ref, ref, fwd_send.at[slot], fwd_recv.at[slot], at_x(to, core))

    def core_copy(d, slot):
        ref = raw.at[4 * core + plus(x, d, 4), :, band(slot)]
        return remote(ref, ref, core_send.at[d, slot], core_recv.at[d, slot], {"co": 1 - core})

    def core_start(d, slot):
        core_copy(d, slot).start()
        drains.append(core_copy(d, slot))

    def send_slot(slot):
        for source in range(4):
            pltpu.make_async_copy(
                cols.at[0, band(slot)], raw.at[group, source, band(slot)], slice_recv.at[slot, source]
            ).wait()
        for way in (0, 1):
            z_start(1, way, slot)

    def send_ring(slot):
        for way in (0, 1):
            ring_copy(way, slot).start()
            drains.append(ring_copy(way, slot))
        core_start(0, slot)

    def pass_ring(slot):
        ring_copy(0, slot).wait_recv()
        if slot < 2:
            fwd_copy(slot).start()
        core_start(3, slot)
        ring_copy(1, slot).wait_recv()
        if slot >= 2:
            fwd_copy(slot).start()
        core_start(1, slot)
        drains.append(fwd_copy(slot))

    def pass_far(slot):
        fwd_copy(slot).wait_recv()
        core_start(2, slot)

    sum_copies = [
        remote(sums, far_sums.at[d - 1], sum_send.at[d - 1], sum_recv.at[d - 1], {"y": plus(y, d, 4)})
        for d in (1, 2, 3)
    ]

    send_slices(0)
    send_surplus()

    cohorts = lax.broadcasted_iota(jnp.int32, (COHORTS, ROWS), 0).astype(F32)
    totals = None
    for first, count, labels in ((0, ROWS, labs[0]), (ROWS, SURPLUS, labs[2])):
        hot = jnp.where(labels == cohorts, 1.0, 0.0).astype(F32)[:, :count]
        hots = jnp.concatenate([hot, hot], axis=0).astype(BF16)
        value = own[first : first + count, :]
        wide = value.astype(F32)
        square = wide * wide
        high = square.astype(BF16)
        low = (square - high.astype(F32)).astype(BF16)
        dots = [jnp.dot(hots, v, preferred_element_type=F32)[:COHORTS] for v in (value, high, low)]
        members = jnp.broadcast_to(jnp.sum(hot, axis=1, keepdims=True), (COHORTS, PANEL))
        part = jnp.concatenate([dots[0], dots[1] + dots[2], members], axis=0)
        totals = part if totals is None else totals + part
    for s in range(4):
        slice_sums[s] = totals[:, s * LANES : (s + 1) * LANES]
    send_row_sums()
    send_slot(0)
    for slot in (1, 2, 3):
        fill_slot(slot)
    send_labels()
    send_ring(0)
    for slot in (1, 2, 3):
        send_slot(slot)
        send_ring(slot)
    for source in range(4):
        pltpu.make_async_copy(slice_sums.at[0], row_sums.at[source], rowsum_recv.at[source]).wait()
    sums[...] = row_sums[0] + row_sums[1] + row_sums[2] + row_sums[3]
    for copy in sum_copies:
        copy.start()
        drains.append(copy)
    z_pass(1, 0)
    z_pass(1, 1)
    pass_ring(0)
    z_pass(1, 2)
    pass_ring(1)
    z_pass(1, 3)

    for copy in sum_copies:
        copy.wait_recv()
    total = sums[...] + far_sums[0] + far_sums[1] + far_sums[2]
    size = total[16:24]
    mean = total[0:8] / size
    var = total[8:16] / size - mean * mean + EPSILON
    spread = lax.rsqrt(var)
    spread = spread * (1.5 - 0.5 * var * spread * spread)
    weight = jnp.zeros((COHORTS, LANES), F32)
    all_weights = jnp.float32(0.0)
    labels = lax.broadcasted_iota(jnp.int32, (COHORTS, LANES), 0)
    for c in range(COHORTS):
        w = weights[c].astype(F32)
        all_weights = all_weights + w
        weight = jnp.where(labels == c, w, weight)
    multiplier = spread * jnp.sqrt(weight / all_weights / size)
    row_tab[group] = jnp.concatenate([mean, multiplier], axis=0)

    def rowtab_copy(d, c):
        ref = row_tab.at[group]
        return remote(
            ref, ref, rowtab_send.at[2 * d + c], rowtab_recv.at[2 * d + c],
            at_x(plus(x, d, 4), plus(core, c, 2)),
        )

    def ztab_copy(step, way):
        at = plus(z, (9 - step) if way == 0 else (step - 1), 8)
        src = row_tab.at[group] if step == 1 else z_tab.at[at]
        return remote(
            src, z_tab.at[at], ztab_send.at[way, step - 1], ztab_recv.at[way, step - 1],
            {"z": plus(z, 1 if way == 0 else 7, 8)},
        )

    def ztab_start(step, way):
        if step < 4 or way == 0:
            ztab_copy(step, way).start()
            drains.append(ztab_copy(step, way))

    def ztab_pass(step):
        for way in (0, 1):
            if step < 4 or way == 0:
                ztab_copy(step, way).wait_recv()
                if step < 4:
                    ztab_start(step + 1, way)

    for d, c in row_peers:
        rowtab_copy(d, c).start()
        drains.append(rowtab_copy(d, c))
    for way in (0, 1):
        ztab_start(1, way)

    z_pass(2, 0)
    pass_ring(2)
    z_pass(2, 1)
    pass_ring(3)
    for source in range(4):
        pltpu.make_async_copy(own_lab, row_labs.at[source], lab_recv.at[source]).wait()
    for source in range(4):
        hot = jnp.where(row_labs[source] == cohorts, 1.0, 0.0).astype(F32)
        hots = jnp.concatenate([hot, hot, hot, jnp.zeros_like(hot)], axis=0)
        hot_ref[source] = hots.T.astype(BF16)
    pass_far(0)
    z_pass(2, 2)
    pass_far(1)
    pass_far(2)
    pass_far(3)
    z_pass(2, 3)
    ztab_pass(1)

    def packed(both):
        mean, multiplier = both[:COHORTS], both[COHORTS:]
        none = jnp.zeros_like(mean)
        return jnp.concatenate([
            jnp.concatenate(list(split_three(mean)) + [none], axis=0),
            jnp.concatenate(list(split_three(multiplier)) + [none], axis=0),
        ], axis=1).astype(BF16)

    def scaled(value, source, table):
        found = jnp.dot(hot_ref[source], table, preferred_element_type=F32)
        return (value.astype(F32) - found[:, :LANES]) * found[:, LANES:]

    for d, c in row_peers:
        rowtab_copy(d, c).wait_recv()
    for d in range(4):
        for slot in range(4):
            core_copy(d, slot).wait_recv()
    z_pass(3, 0)

    def fill_panel(g, carry):
        table = packed(row_tab[g])
        at = pl.ds(pl.multiple_of(g * LANES, LANES), LANES)
        for source in range(4):
            value = scaled(raw[g, source], source, table)
            panel[source * ROWS : (source + 1) * ROWS, at] = value.astype(BF16)
        return carry

    lax.fori_loop(0, 8, fill_panel, 0)

    sign = 1 - 2 * core

    def hops_to(s):
        return lax.rem(sign * (lax.div(s, 2) - y) + 4, 4)

    def half_of(ref, h):
        return ref.at[:, pl.ds(h * PANEL, PANEL)]

    def part_copy(s, h, kind):
        p = lax.rem(s, 2)
        dst, recv, device = {
            "mid": (mid_in.at[p, h], mid_recv.at[p, h], onward),
            "acc": (acc_in.at[p, h], acc_recv.at[p, h], onward),
            "dir": (dir_in.at[p, h], dir_recv.at[p, h], {"y": plus(y, 3 - 2 * core, 4)}),
        }[kind]
        return remote(half_of(partial.at[s], h), dst, part_send.at[s, h], recv, device)

    def make_partial(s, value_of, table):
        table = packed(table)
        for source in range(4):
            value = scaled(value_of(source), source, table)
            turned[:, source * ROWS : (source + 1) * ROWS] = value.T.astype(BF16)
        hops = hops_to(s)
        for h in range(2):
            at = slice(h * PANEL, (h + 1) * PANEL)
            value = jnp.dot(turned[...], panel[:, at], preferred_element_type=F32)
            keep[s, :, at] = value
            partial[s, :, at] = value.astype(BF16)

            @pl.when(hops == 2)
            def _():
                part_copy(s, h, "mid").start()

            @pl.when(hops == 3)
            def _():
                part_copy(s, h, "dir").start()

    def add_relay(s):
        @pl.when(hops_to(s) == 1)
        def _():
            for h in range(2):
                p = lax.rem(s, 2)
                part_copy(s, h, "mid").wait_recv()
                at = slice(h * PANEL, (h + 1) * PANEL)
                partial[s, :, at] = (keep[s, :, at] + mid_in[p, h].astype(F32)).astype(BF16)
                part_copy(s, h, "acc").start()

    def from_z(d):
        s = plus(z, d, 8)
        make_partial(s, lambda source: z_raw[s, source], z_tab[s])

    make_partial(z, lambda source: raw[group, source], row_tab[group])
    z_pass(3, 1)
    from_z(7)
    from_z(1)
    z_pass(3, 2)
    ztab_pass(2)
    z_pass(3, 3)
    from_z(6)
    from_z(2)
    add_relay(z)
    ztab_pass(3)
    from_z(5)
    add_relay(plus(z, 7, 8))
    from_z(3)
    add_relay(plus(z, 1, 8))
    add_relay(plus(z, 6, 8))
    for slot in range(4):
        z_pass(4, slot)
    ztab_pass(4)
    from_z(4)
    add_relay(plus(z, 2, 8))
    add_relay(plus(z, 5, 8))
    add_relay(plus(z, 3, 8))
    add_relay(plus(z, 4, 8))

    def fold_copy(p, h):
        target = 2 * h + p
        d = plus(target, 4 - x, 4) - 1
        return remote(
            folded.at[p, h], out.at[pl.ds(pl.multiple_of(x * LANES, LANES), LANES)],
            fold_send.at[p, h], fold_recv.at[d], at_x(target, core),
        )

    for p in (plus(z, 1, 2), plus(z, 0, 2)):
        for h in range(2):
            s = 2 * y + p
            part_copy(s, h, "acc").wait_recv()
            part_copy(s, h, "dir").wait_recv()
            at = slice(h * PANEL, (h + 1) * PANEL)
            value = keep[s, :, at] + acc_in[p, h].astype(F32) + dir_in[p, h].astype(F32)
            value = value.astype(BF16)

            @pl.when(2 * h + p != x)
            def _():
                folded[p, h] = value
                fold_copy(p, h).start()

            @pl.when(2 * h + p == x)
            def _():
                out[pl.ds(pl.multiple_of(x * LANES, LANES), LANES), :] = value

    for d in (1, 2, 3):
        pltpu.make_async_copy(
            folded.at[0, 0], out.at[pl.ds(0, LANES)], fold_recv.at[d - 1]
        ).wait()

    for copy in drains:
        copy.wait_send()

    @pl.when(xh != core)
    def _():
        for slot in range(4):
            slice_copy(slot, 0).wait_send()
        lab_copy(0).wait_send()
        rowsum_copy(0).wait_send()

    for s in range(8):
        @pl.when(y != s // 2)
        def _():
            for h in range(2):
                part_copy(jnp.int32(s), h, "dir").wait_send()

    for p in range(2):
        for h in range(2):
            @pl.when(2 * h + p != x)
            def _():
                fold_copy(p, h).wait_send()


def shards(dosage, cohort, live_blocks, weight_counts):
    slot = lax.broadcasted_iota(jnp.int32, cohort.shape, 0) // BLOCK
    code = jnp.where(slot < live_blocks[0], cohort, -1).astype(F32).reshape(7, BLOCK)
    none = jnp.full((BLOCK,), -1.0, F32)
    labs = jnp.stack([
        jnp.concatenate([code[0], code[1], code[2], code[3]]),
        jnp.concatenate([none, code[6], code[5], code[4]]),
        jnp.concatenate([code[4], code[5], code[6], none]),
    ])
    labs = jnp.broadcast_to(labs[:, None, :], (3, COHORTS, ROWS))
    vmem = pl.BlockSpec(memory_space=pltpu.VMEM)
    smem = pl.BlockSpec(memory_space=pltpu.SMEM)

    def dma(*shape):
        return pltpu.SemaphoreType.DMA(shape)

    ld = pl.pallas_call(
        kernel,
        out_shape=jax.ShapeDtypeStruct((PANEL, PANEL), BF16),
        in_specs=[pl.BlockSpec(memory_space=pl.ANY), vmem, smem, smem],
        out_specs=vmem,
        scratch_shapes=[
            pltpu.VMEM((ROWS + SURPLUS, PANEL), BF16),
            pltpu.VMEM((3, BLOCK, PANEL), BF16),
            pltpu.VMEM((COHORTS, ROWS), F32),
            pltpu.VMEM((COHORTS, ROWS), F32),
            pltpu.VMEM((4, ROWS, LANES), BF16),
            pltpu.VMEM((8, 4, ROWS, LANES), BF16),
            pltpu.VMEM((4, COHORTS, ROWS), F32),
            pltpu.VMEM((4, ROWS, 32), BF16),
            pltpu.VMEM((4, 24, LANES), F32),
            pltpu.VMEM((4, 24, LANES), F32),
            pltpu.VMEM((24, LANES), F32),
            pltpu.VMEM((3, 24, LANES), F32),
            pltpu.VMEM((8, 16, LANES), F32),
            pltpu.VMEM((8, 16, LANES), F32),
            pltpu.VMEM((8, 4, ROWS, LANES), BF16),
            pltpu.VMEM((DEPTH, WIDTH), BF16),
            pltpu.VMEM((LANES, DEPTH), BF16),
            pltpu.VMEM((8, LANES, WIDTH), F32),
            pltpu.VMEM((8, LANES, WIDTH), BF16),
            pltpu.VMEM((2, 2, LANES, PANEL), BF16),
            pltpu.VMEM((2, 2, LANES, PANEL), BF16),
            pltpu.VMEM((2, 2, LANES, PANEL), BF16),
            pltpu.VMEM((2, 2, LANES, PANEL), BF16),
            pltpu.SemaphoreType.DMA, dma(3), dma(3),
            pltpu.SemaphoreType.DMA, pltpu.SemaphoreType.DMA,
            dma(4, 4), dma(4, 4), dma(4), dma(4), dma(4), dma(4), dma(3), dma(3),
            dma(8), dma(8), dma(2, 4), dma(2, 4),
            dma(2, 4), dma(2, 4), dma(4), dma(4), dma(4, 4), dma(4, 4),
            dma(2, 4, 4), dma(2, 4, 4), dma(8, 2), dma(2, 2), dma(2, 2), dma(2, 2),
            dma(2, 2), dma(3),
        ],
        compiler_params=pltpu.CompilerParams(
            collective_id=0, has_side_effects=True, vmem_limit_bytes=60 * 1024 * 1024
        ),
    )(dosage, labs, live_blocks, weight_counts)
    return ld.astype(F32)


def solution(mesh):
    torus = Mesh(mesh.devices.reshape(4, 2, 2, 8, 2), ("y", "xl", "co", "z", "xh"))
    samp, var = ("y", "xl", "co"), ("z", "xh")
    placed = (P(samp, var), P(samp), P(samp), P())
    return jax.shard_map(
        shards, mesh=torus, in_specs=placed, out_specs=P(samp, var), check_vma=False
    )
```
